512 devices in a mesh: cross: 16 (over y_hi, x, core), along: 32 (over z, y_lo).
Axes of the slice: x: 4, y: 4 (y_hi: 2, y_lo: 2; y = y_hi * 2 + y_lo), z: 16, core: 2. Of those that a mesh axis runs over, the one named last changes fastest.
Arguments:
- surface: float32 [4096, 8192], P('cross', 'along'), may hold values from -6 to 6
- flux_cross: float32 [4096, 8192], P('cross', 'along'), may hold values from -6 to 6
- flux_along: float32 [4096, 8192], P('cross', 'along'), may hold values from -6 to 6
- celerity_sq: float32 [4096, 8192], P('cross', 'along'), may hold values from 0.05 to 1
- wet_mask: int32 [4096, 8192], P('cross', 'along'), may hold values from 0 to 1, as said below
- range_test: float32 [8192, 128], P('along'), may hold values from -0.0625 to 0.0625
- corange_test: float32 [128, 4096], P(None, 'cross'), may hold values from -0.09375 to 0.09375
- core_left: float32 [256, 4096], P(None, 'cross'), may hold values from -0.09375 to 0.09375
- core_right: float32 [8192, 256], P('along'), may hold values from -0.0625 to 0.0625
Outputs:
- surface_next: float32 [4096, 8192], P('cross', 'along')
- flux_cross_next: float32 [4096, 8192], P('cross', 'along')
- flux_along_next: float32 [4096, 8192], P('cross', 'along')
- range_sketch: float32 [4096, 128], P('cross')
- corange_sketch: float32 [128, 8192], P(None, 'along')
- core_sketch: float32 [256, 256], replicated
The draws below stay inside these ranges and needn't reach their ends.
Inputs may be any that keep to these rules, and one draw needn't show every extreme that they name: `wet_mask`: 1 marks a wet cell, 0 a dry one.
All inputs are finite; a program needn't handle non-finite values.
Results may differ from the reference program's by a relative error of at most 0.000073.
Values sent between devices are 32-bit elements; how exact they have to be, the bound alone decides.
A program may use at most 64 MiB of HBM per device.

```python
import math
import jax
import jax.numpy as jnp
from jax import lax

K = 128
S = 256
NX = 4096
NY = 8192


def draw_wet_mask(key, part):
    rows = lax.broadcasted_iota(jnp.int32, (NX, NY), 0)
    limit = 250 + 500 * rows // NX
    picks = jax.random.randint(key, (NX, NY), 0, 1000, dtype=jnp.int32)
    return jnp.where(picks < limit, 1, 0).astype(jnp.int32)


def steps_of(rng, dims, shards, smallest, largest):
    gain = 1.0
    for dim, parts in shards:
        steps = jax.random.uniform(jax.random.fold_in(jax.random.fold_in(rng, 6), dim), (parts,), jnp.float32, smallest / len(shards), largest / len(shards))
        gain = gain * jnp.repeat(jnp.exp(steps), dims[dim] // parts).reshape((-1,) + (1,) * (len(dims) - 1 - dim))
    return gain


def scatter_about(rng, extent, scale, most, cuts=(), kind=jnp.bfloat16):
    values = scale * jax.random.normal(rng, extent, jnp.float32)
    if cuts:
        values = values * steps_of(rng, extent, cuts, -0.22, 0.18)
    return jnp.clip(values, -most, most).astype(kind)


def setup_inputs(seed: int = 0) -> dict:
    key_of = jax.random.split(jax.random.key(seed), 10)
    surface = scatter_about(key_of[0], (NX, NY), 1.0, 6.0, ((0, 16), (1, 32)), jnp.float32)
    flux_cross = scatter_about(key_of[1], (NX, NY), 1.0, 6.0, ((0, 16), (1, 32)), jnp.float32)
    flux_along = scatter_about(key_of[2], (NX, NY), 1.0, 6.0, ((0, 16), (1, 32)), jnp.float32)
    celerity_sq = jnp.clip(jnp.exp(math.log(1.0) - 2.9957323 * jax.random.uniform(key_of[3], (NX, NY), jnp.float32) ** steps_of(key_of[3], (NX, NY), ((0, 16), (1, 32)), -0.2, 0.2)), 0.05, 1.0)
    wet_mask = draw_wet_mask(jax.random.fold_in(key_of[9], 71), 0)
    range_test = scatter_about(key_of[5], (NY, K), NY ** -0.5, 0.0625, ((0, 32),), jnp.float32)
    corange_test = scatter_about(key_of[6], (K, NX), NX ** -0.5, 0.09375, ((1, 16),), jnp.float32)
    core_left = scatter_about(key_of[7], (S, NX), NX ** -0.5, 0.09375, ((1, 16),), jnp.float32)
    core_right = scatter_about(key_of[8], (NY, S), NY ** -0.5, 0.0625, ((0, 32),), jnp.float32)
    return dict(surface=surface, flux_cross=flux_cross, flux_along=flux_along, celerity_sq=celerity_sq, wet_mask=wet_mask, range_test=range_test, corange_test=corange_test, core_left=core_left, core_right=core_right)


def centred(field, axis):
    widths = [(0, 0), (0, 0)]
    widths[axis] = (2, 2)
    padded = jnp.pad(field, widths)
    count = field.shape[axis]

    def part(start):
        return lax.slice_in_dim(padded, start, start + count, axis=axis)

    return (8.0 * (part(3) - part(1)) - (part(4) - part(0))) / 12.0


def tendency(elev, flux_x, flux_y, wet, celerity_sq):
    masked_x = wet * flux_x
    masked_y = wet * flux_y
    d_elev = -0.25 * wet * (centred(masked_x, 0) + centred(masked_y, 1))
    friction = 0.02 / celerity_sq
    d_flux_x = -wet * (0.25 * celerity_sq * centred(elev, 0) + friction * flux_x)
    d_flux_y = -wet * (0.25 * celerity_sq * centred(elev, 1) + friction * flux_y)
    return d_elev, d_flux_x, d_flux_y


def reference(surface, flux_cross, flux_along, celerity_sq, wet_mask, range_test, corange_test, core_left, core_right):
    wet = wet_mask.astype(jnp.float32)
    k1e, k1p, k1q = tendency(surface, flux_cross, flux_along, wet, celerity_sq)
    k2e, k2p, k2q = tendency(surface + k1e, flux_cross + k1p, flux_along + k1q, wet, celerity_sq)
    surface_next = surface + 0.5 * (k1e + k2e)
    flux_cross_next = flux_cross + 0.5 * (k1p + k2p)
    flux_along_next = flux_along + 0.5 * (k1q + k2q)
    high = lax.Precision.HIGHEST
    range_sketch = jnp.dot(surface_next, range_test, precision=high, preferred_element_type=jnp.float32)
    corange_sketch = jnp.dot(corange_test, surface_next, precision=high, preferred_element_type=jnp.float32)
    right_rows = jnp.dot(surface_next, core_right, precision=high, preferred_element_type=jnp.float32)
    core_sketch = jnp.dot(core_left, right_rows, precision=high, preferred_element_type=jnp.float32)
    return surface_next, flux_cross_next, flux_along_next, range_sketch, corange_sketch, core_sketch
```

```python
import functools

import jax
import jax.numpy as jnp
from jax import lax
from jax.experimental import pallas as pl
from jax.experimental.pallas import tpu as pltpu
from jax.sharding import PartitionSpec as P

MESH = pl.DeviceIdType.MESH
F32 = jnp.float32
BF16 = jnp.bfloat16
NC = 16
NA = 32
NZ = 16
ALPHA = 0.25 / 12.0
CH = 32


def split(x):
    hi = x.astype(BF16)
    return hi, (x - hi.astype(F32)).astype(BF16)


def dot3(a, b):
    dot = functools.partial(jnp.dot, preferred_element_type=F32)
    (ah, al), (bh, bl) = a, b
    return dot(ah, bh) + (dot(ah, bl) + dot(al, bh))


def d12(f, axis):
    n = f.shape[axis]
    up1, dn1 = pltpu.roll(f, n - 1, axis), pltpu.roll(f, 1, axis)
    up2, dn2 = pltpu.roll(f, n - 2, axis), pltpu.roll(f, 2, axis)
    return 8.0 * (up1 - dn1) - (up2 - dn2)


def kernel(
    e_in, p_in, q_in, c_in, w_in, om_in, th_in, l_in, r_in,
    e_out, p_out, q_out, rng_out, cor_out, core_out,
    fld, wid, tsl, asl, bsl, xs, xb, sph, wpx, e1x, sv, shl, pv, qv,
    om, th, lm, rm, omh, thh, lmh, rmh, trh,
    rpart, cpart, kpart, rrec, crec, krec, zrec, rsum, csum, ksum, zsum,
    in_sem, out_sem, row_s, row_r, col_s, col_r, cor_s, cor_r,
    rs_s, rs_r, ag_s, ag_r,
):
    cross = lax.axis_index("cross")
    along = lax.axis_index("along")
    z, ylo = along // 2, along % 2
    plane = ylo * NC + cross

    loads = [
        pltpu.make_async_copy(src, fld.at[k, pl.ds(8, 256)], in_sem.at[k])
        for k, src in enumerate((e_in, p_in, q_in, c_in))
    ]
    loads.append(pltpu.make_async_copy(w_in, wid.at[pl.ds(8, 256)], in_sem.at[4]))
    for copy in loads:
        copy.start()
    mats = [
        pltpu.make_async_copy(src, dst, in_sem.at[5 + k])
        for k, (src, dst) in enumerate(((om_in, om), (th_in, th), (l_in, lm), (r_in, rm)))
    ]
    for copy in mats:
        copy.start()

    def along_peer(d):
        return {"cross": cross, "along": (along + d) % NA}

    def cross_peer(d):
        return {"cross": (cross + d) % NC, "along": along}

    def plane_peer(d):
        k = (plane + d) % NA
        return {"cross": k % NC, "along": z * 2 + k // NC}

    def z_peer(d):
        return {"cross": cross, "along": ((z + d) % NZ) * 2 + ylo}

    barrier = pltpu.get_barrier_semaphore()

    @pl.loop(1, NA)
    def _(d):
        pl.semaphore_signal(barrier, inc=1, device_id=along_peer(d), device_id_type=MESH)

    @pl.loop(1, NA)
    def _(d):
        pl.semaphore_signal(barrier, inc=1, device_id=plane_peer(d), device_id_type=MESH)

    for copy in loads:
        copy.wait()

    lane = lax.broadcasted_iota(jnp.int32, (128, 128), 1)
    for b in range(2):
        rows = pl.ds(8 + 128 * b, 128)
        fields = [wid[rows].astype(F32)] + [fld[k, rows] for k in (1, 2, 0, 3)]
        slab = jnp.zeros((128, 128), F32)
        for k, f in enumerate(fields):
            x = jnp.where(lane < 64, f[:, :128], f[:, 128:])
            x = pltpu.roll(x, 16 * k + 8, 1)
            slab = jnp.where((lane >= 16 * k) & (lane < 16 * k + 16), x, slab)
        tsl[:, :, :, pl.ds(128 * b, 128)] = slab.T.reshape(8, 2, 8, 128)

    @pl.when(along == NA - 1)
    def _():
        tsl[0, 0] = jnp.zeros((8, 256), F32)
        tsl[3, 0] = jnp.zeros((8, 256), F32)

    @pl.when(along == 0)
    def _():
        tsl[0, 1] = jnp.zeros((8, 256), F32)
        tsl[3, 1] = jnp.zeros((8, 256), F32)

    asl[5:8] = jnp.zeros((3, 2, 8, 256), F32)
    for side in range(2):
        bsl[side, 3:8] = jnp.zeros((5, 2, 8, 128), F32)

    pl.semaphore_wait(barrier, 2 * (NA - 1))

    halo = []
    for k in range(5):
        ref = wid if k == 4 else fld.at[k]
        for side, (src, dst, step) in enumerate(((256, 0, 1), (8, 264, NC - 1))):
            halo.append(
                pltpu.make_async_remote_copy(
                    src_ref=ref.at[pl.ds(src, 8)],
                    dst_ref=ref.at[pl.ds(dst, 8)],
                    send_sem=row_s.at[2 * k + side],
                    recv_sem=row_r.at[2 * k + side],
                    device_id=cross_peer(step),
                    device_id_type=MESH,
                )
            )
    cols = []
    for side, step in enumerate((1, NA - 1)):
        cols.append(
            pltpu.make_async_remote_copy(
                src_ref=tsl.at[pl.ds(0, 5), side],
                dst_ref=asl.at[pl.ds(0, 5), side],
                send_sem=col_s.at[side],
                recv_sem=col_r.at[side],
                device_id=along_peer(step),
                device_id_type=MESH,
            )
        )
    for copy in cols + halo:
        copy.start()

    for copy in mats:
        copy.wait()
    for src, dst in ((om, omh), (th, thh), (lm, lmh), (rm, rmh)):
        hi, lo = split(src[...])
        dst[0] = hi
        dst[1] = lo

    for copy in cols:
        copy.wait_recv()

    corners = []
    for side, step in enumerate((1, NC - 1)):
        corners.append(
            pltpu.make_async_remote_copy(
                src_ref=asl.at[pl.ds(0, 3), :, :, pl.ds(128 * (1 - side), 128)],
                dst_ref=bsl.at[side, pl.ds(0, 3)],
                send_sem=cor_s.at[side],
                recv_sem=cor_r.at[side],
                device_id=cross_peer(step),
                device_id_type=MESH,
            )
        )
    for copy in corners:
        copy.start()

    for b in range(2):
        xs[pl.ds(128 * b, 128)] = asl[:, :, :, pl.ds(128 * b, 128)].reshape(128, 128).T

    for copy in halo:
        copy.wait_recv()

    @pl.when(cross == 0)
    def _():
        fld[0, pl.ds(0, 8)] = jnp.zeros((8, 256), F32)
        wid[pl.ds(0, 8)] = jnp.zeros((8, 256), jnp.int32)

    @pl.when(cross == NC - 1)
    def _():
        fld[0, pl.ds(264, 8)] = jnp.zeros((8, 256), F32)
        wid[pl.ds(264, 8)] = jnp.zeros((8, 256), jnp.int32)

    def beside(x, k):
        return pltpu.roll(x, 128 - (16 * k + 8), 1)

    def sp_rows(r, n, lead):
        w = wid[pl.ds(r, n)].astype(F32)
        wp = w * fld[1, pl.ds(r, n)]
        c = fld[3, pl.ds(r, n)]
        e = fld[0, pl.ds(pl.multiple_of(r - lead, 8), n + 16)]
        de = d12(e, 0)[lead : lead + n]
        wpx[pl.ds(r, n)] = wp
        sph[pl.ds(r, n)] = 2.0 * wp - w * c * ALPHA * de - (0.02 / c) * wp

    @pl.loop(0, 256 // CH)
    def _(i):
        sp_rows(pl.multiple_of(8 + i * CH, 8), CH, 8)

    sp_rows(0, 8, 0)
    sp_rows(264, 8, 16)

    @pl.loop(0, 256 // CH)
    def _(i):
        r0 = pl.multiple_of(i * CH, 8)
        r = pl.multiple_of(8 + i * CH, 8)
        own = pl.ds(r, CH)
        x = xs[pl.ds(r0, CH)]
        wt = wid[own].astype(F32)
        e0 = fld[0, own]
        w = jnp.concatenate([wt, beside(x, 0)], axis=1)
        q = jnp.concatenate([fld[2, own], beside(x, 2)], axis=1)
        e = jnp.concatenate([e0, beside(x, 3)], axis=1)
        c = jnp.concatenate([fld[3, own], beside(x, 4)], axis=1)
        wq = w * q
        sq = 2.0 * wq - w * c * ALPHA * d12(e, 1) - (0.02 / c) * wq
        dy = d12(sq, 1)[:, :256]
        s = sph[pl.ds(pl.multiple_of(r - 8, 8), CH + 16)]
        dx = d12(s, 0)[8 : 8 + CH]
        en = e0 - (0.5 * ALPHA) * wt * (dx + dy)
        sv[pl.ds(r0, CH)] = en
        hi, lo = split(en)
        shl[0, pl.ds(r0, CH)] = hi
        shl[1, pl.ds(r0, CH)] = lo

    outs = [pltpu.make_async_copy(sv, e_out, out_sem.at[0])]
    outs[0].start()

    def send(n, peer, src, dst, phase, s_sem, r_sem):
        @pl.loop(0, n - 1)
        def _(s):
            half = (s + 1) // 2
            d = n // 2 + (1 - 2 * (s % 2)) * half
            pltpu.make_async_remote_copy(
                src_ref=src(d),
                dst_ref=dst(d),
                send_sem=s_sem.at[phase],
                recv_sem=r_sem.at[phase],
                device_id=peer(d),
                device_id_type=MESH,
            ).start()

    def await_recv(ref, sem):
        pltpu.make_async_copy(ref, ref, sem).wait()

    surf = (shl[0], shl[1])
    rpart[...] = dot3(surf, (omh[0], omh[1])).reshape(NA, 8, 128)
    send(NA, along_peer, lambda d: rpart.at[(along + d) % NA], lambda d: rrec.at[d], 0, rs_s, rs_r)
    tr = dot3(surf, (rmh[0], rmh[1]))
    hi, lo = split(tr)
    trh[0] = hi
    trh[1] = lo
    kpart[...] = dot3((lmh[0], lmh[1]), (trh[0], trh[1])).reshape(NA, 8, 256)
    send(NA, plane_peer, lambda d: kpart.at[(plane + d) % NA], lambda d: krec.at[d], 1, rs_s, rs_r)
    cpart[...] = dot3((thh[0], thh[1]), surf).reshape(NC, 8, 256)
    send(NC, cross_peer, lambda d: cpart.at[(cross + d) % NC], lambda d: crec.at[d], 2, rs_s, rs_r)

    for copy in corners:
        copy.wait_recv()

    @pl.when(cross == 0)
    def _():
        bsl[0] = jnp.zeros((8, 2, 8, 128), F32)

    @pl.when(cross == NC - 1)
    def _():
        bsl[1] = jnp.zeros((8, 2, 8, 128), F32)

    for side in range(2):
        t = bsl[side, pl.ds(0, 8)].reshape(128, 128).T
        xb[pl.ds(8 * side, 8)] = t[120:128] if side == 0 else t[0:8]

    def e1_rows(r, n, x, lead):
        w = wid[pl.ds(r, n)].astype(F32)
        wq = jnp.concatenate(
            [w * fld[2, pl.ds(r, n)], beside(x, 0) * beside(x, 2)], axis=1
        )
        wp = wpx[pl.ds(pl.multiple_of(r - lead, 8), n + 16)]
        dx = d12(wp, 0)[lead : lead + n]
        dy = d12(wq, 1)[:, :256]
        e = fld[0, pl.ds(r, n)]
        return e + (e - ALPHA * w * (dx + dy))

    @pl.loop(0, 256 // CH)
    def _(i):
        r = pl.multiple_of(8 + i * CH, 8)
        e1x[pl.ds(r, CH)] = e1_rows(r, CH, xs[pl.ds(pl.multiple_of(i * CH, 8), CH)], 8)

    e1x[pl.ds(0, 8)] = e1_rows(0, 8, xb[pl.ds(0, 8)], 0)
    e1x[pl.ds(264, 8)] = e1_rows(264, 8, xb[pl.ds(8, 8)], 16)

    xb[pl.ds(16, 256)] = xs[...]

    @pl.loop(0, 256 // CH)
    def _(i):
        r0 = pl.multiple_of(i * CH, 8)
        r = pl.multiple_of(8 + i * CH, 8)
        own = pl.ds(r, CH)
        x = xs[pl.ds(r0, CH)]
        w = wid[own].astype(F32)
        c = fld[3, own]
        p, q = fld[1, own], fld[2, own]
        wc = w * c * ALPHA
        fr = w * (0.02 / c)
        p1 = p - wc * d12(fld[0, pl.ds(r0, CH + 16)], 0)[8 : 8 + CH] - fr * p
        ee = e1x[pl.ds(r0, CH + 16)]
        dx = d12(ee, 0)[8 : 8 + CH]
        pv[pl.ds(r0, CH)] = p - 0.5 * (wc * dx + fr * (p + p1))

        hb = jnp.concatenate(
            [
                jnp.where(i == 0, xb[pl.ds(0, 8)], xb[pl.ds(pl.multiple_of(jnp.maximum(r0 + 8, 8), 8), 8)]),
                x,
                jnp.where(
                    i == 256 // CH - 1,
                    xb[pl.ds(8, 8)],
                    xb[pl.ds(pl.multiple_of(jnp.minimum(r0 + 16 + CH, 264), 8), 8)],
                ),
            ],
            axis=0,
        )
        wpb = beside(hb, 0) * beside(hb, 1)
        dxb = d12(wpb, 0)[8 : 8 + CH]
        wb = beside(x, 0)
        wq = jnp.concatenate([w * q, wb * beside(x, 2)], axis=1)
        dyb = d12(wq, 1)[:, 256:]
        eb = beside(x, 3)
        e1b = eb + (eb - ALPHA * wb * (dxb + dyb))
        e = jnp.concatenate([fld[0, own], eb], axis=1)
        q1 = q - wc * d12(e, 1)[:, :256] - fr * q
        dy = d12(jnp.concatenate([e1x[own], e1b], axis=1), 1)[:, :256]
        qv[pl.ds(r0, CH)] = q - 0.5 * (wc * dy + fr * (q + q1))

    outs += [
        pltpu.make_async_copy(pv, p_out, out_sem.at[1]),
        pltpu.make_async_copy(qv, q_out, out_sem.at[2]),
    ]
    outs[1].start()
    outs[2].start()

    await_recv(krec.at[pl.ds(1, NA - 1)], rs_r.at[1])
    krec[0] = kpart[plane]
    ksum[...] = jnp.sum(krec[...], axis=0)
    send(NZ, z_peer, lambda d: ksum, lambda d: zrec.at[d], 3, rs_s, rs_r)

    await_recv(crec.at[pl.ds(1, NC - 1)], rs_r.at[2])
    crec[0] = cpart[cross]
    csum[pl.ds(pl.multiple_of(8 * cross, 8), 8)] = jnp.sum(crec[...], axis=0)
    mine = pl.ds(pl.multiple_of(8 * cross, 8), 8)
    send(NC, cross_peer, lambda d: csum.at[mine], lambda d: csum.at[mine], 2, ag_s, ag_r)

    await_recv(rrec.at[pl.ds(1, NA - 1)], rs_r.at[0])
    rrec[0] = rpart[along]
    own_r = pl.ds(pl.multiple_of(8 * along, 8), 8)
    rsum[own_r] = jnp.sum(rrec[...], axis=0)
    send(NA, along_peer, lambda d: rsum.at[own_r], lambda d: rsum.at[own_r], 0, ag_s, ag_r)

    await_recv(zrec.at[pl.ds(1, NZ - 1)], rs_r.at[3])
    zrec[0] = ksum[...]
    total = zrec[z]
    for k in range(1, NZ):
        total = total + zrec[(z - k + NZ) % NZ]
    own_k = pl.ds(pl.multiple_of(8 * plane, 8), 8)
    zsum[own_k] = total
    send(NA, plane_peer, lambda d: zsum.at[own_k], lambda d: zsum.at[own_k], 1, ag_s, ag_r)

    await_recv(csum.at[pl.ds(0, 120)], ag_r.at[2])
    outs.append(pltpu.make_async_copy(csum, cor_out, out_sem.at[4]))
    outs[-1].start()
    await_recv(rsum.at[pl.ds(0, 248)], ag_r.at[0])
    outs.append(pltpu.make_async_copy(rsum, rng_out, out_sem.at[3]))
    outs[-1].start()
    await_recv(zsum.at[pl.ds(0, 248)], ag_r.at[1])
    outs.append(pltpu.make_async_copy(zsum, core_out, out_sem.at[5]))
    outs[-1].start()

    for copy in halo + cols + corners:
        copy.wait_send()
    await_recv(rrec.at[pl.ds(1, NA - 1)], rs_s.at[0])
    await_recv(krec.at[pl.ds(1, NA - 1)], rs_s.at[1])
    await_recv(crec.at[pl.ds(1, NC - 1)], rs_s.at[2])
    await_recv(zrec.at[pl.ds(1, NZ - 1)], rs_s.at[3])
    await_recv(rsum.at[pl.ds(0, 248)], ag_s.at[0])
    await_recv(zsum.at[pl.ds(0, 248)], ag_s.at[1])
    await_recv(csum.at[pl.ds(0, 120)], ag_s.at[2])
    for copy in outs:
        copy.wait()


def body(*args):
    vm = pltpu.VMEM
    dma = pltpu.SemaphoreType.DMA
    sds = jax.ShapeDtypeStruct
    return pl.pallas_call(
        kernel,
        out_shape=(
            sds((256, 256), F32),
            sds((256, 256), F32),
            sds((256, 256), F32),
            sds((256, 128), F32),
            sds((128, 256), F32),
            sds((256, 256), F32),
        ),
        in_specs=[pl.BlockSpec(memory_space=pl.ANY)] * 9,
        out_specs=[pl.BlockSpec(memory_space=pl.ANY)] * 6,
        scratch_shapes=[
            vm((4, 272, 256), F32),
            vm((272, 256), jnp.int32),
            vm((8, 2, 8, 256), F32),
            vm((8, 2, 8, 256), F32),
            vm((2, 8, 2, 8, 128), F32),
            vm((256, 128), F32),
            vm((272, 128), F32),
            vm((272, 256), F32),
            vm((272, 256), F32),
            vm((272, 256), F32),
            vm((256, 256), F32),
            vm((2, 256, 256), BF16),
            vm((256, 256), F32),
            vm((256, 256), F32),
            vm((256, 128), F32),
            vm((128, 256), F32),
            vm((256, 256), F32),
            vm((256, 256), F32),
            vm((2, 256, 128), BF16),
            vm((2, 128, 256), BF16),
            vm((2, 256, 256), BF16),
            vm((2, 256, 256), BF16),
            vm((2, 256, 256), BF16),
            vm((NA, 8, 128), F32),
            vm((NC, 8, 256), F32),
            vm((NA, 8, 256), F32),
            vm((NA, 8, 128), F32),
            vm((NC, 8, 256), F32),
            vm((NA, 8, 256), F32),
            vm((NZ, 8, 256), F32),
            vm((256, 128), F32),
            vm((128, 256), F32),
            vm((8, 256), F32),
            vm((256, 256), F32),
            dma((9,)),
            dma((6,)),
            dma((10,)),
            dma((10,)),
            dma((2,)),
            dma((2,)),
            dma((2,)),
            dma((2,)),
            dma((4,)),
            dma((4,)),
            dma((3,)),
            dma((3,)),
        ],
        compiler_params=pltpu.CompilerParams(collective_id=0, has_side_effects=True),
    )(*args)


def solution(mesh):
    return jax.shard_map(
        body,
        mesh=mesh,
        in_specs=(
            P("cross", "along"),
            P("cross", "along"),
            P("cross", "along"),
            P("cross", "along"),
            P("cross", "along"),
            P("along", None),
            P(None, "cross"),
            P(None, "cross"),
            P("along", None),
        ),
        out_specs=(
            P("cross", "along"),
            P("cross", "along"),
            P("cross", "along"),
            P("cross", None),
            P(None, "along"),
            P(),
        ),
        check_vma=False,
    )
```

```python
import functools

import jax
import jax.numpy as jnp
from jax import lax
from jax.experimental import pallas as pl
from jax.experimental.pallas import tpu as pltpu
from jax.sharding import PartitionSpec as P

MESH = pl.DeviceIdType.MESH
F32 = jnp.float32
BF16 = jnp.bfloat16
NC = 16
NA = 32
NZ = 16
ALPHA = 0.25 / 12.0
CH = 32


def split(x):
    hi = x.astype(BF16)
    return hi, (x - hi.astype(F32)).astype(BF16)


def dot3(a, b):
    dot = functools.partial(jnp.dot, preferred_element_type=F32)
    (ah, al), (bh, bl) = a, b
    return dot(ah, bh) + (dot(ah, bl) + dot(al, bh))


def d12(f, axis):
    n = f.shape[axis]
    up1, dn1 = pltpu.roll(f, n - 1, axis), pltpu.roll(f, 1, axis)
    up2, dn2 = pltpu.roll(f, n - 2, axis), pltpu.roll(f, 2, axis)
    return 8.0 * (up1 - dn1) - (up2 - dn2)


def kernel(
    e_in, p_in, q_in, c_in, w_in, om_in, th_in, l_in, r_in,
    sv, pv, qv, rsum, csum, zsum,
    fld, wid, tsl, asl, bsl, xs, xb, sph, wpx, e1x, shl,
    om, th, lm, rm, omh, thh, lmh, rmh,
    rpart, cpart, kpart, rrec, crec, krec, zrec, ksum,
    in_sem, row_s, row_r, col_s, col_r, cor_s, cor_r,
    rs_s, rs_r, ag_s, ag_r, near,
):
    cross = lax.axis_index("cross")
    along = lax.axis_index("along")
    z, ylo = along // 2, along % 2
    plane = ylo * NC + cross

    loads = [
        pltpu.make_async_copy(src, fld.at[k, pl.ds(8, 256)], in_sem.at[k])
        for k, src in enumerate((e_in, p_in, q_in, c_in))
    ]
    loads.append(pltpu.make_async_copy(w_in, wid.at[pl.ds(8, 256)], in_sem.at[4]))
    for copy in loads:
        copy.start()
    mats = [
        pltpu.make_async_copy(src, dst, in_sem.at[5 + k])
        for k, (src, dst) in enumerate(((om_in, om), (th_in, th), (l_in, lm), (r_in, rm)))
    ]
    for copy in mats:
        copy.start()

    rem = lax.rem

    def along_peer(d):
        return {"cross": cross, "along": rem(along + d, NA)}

    def cross_peer(d):
        return {"cross": rem(cross + d, NC), "along": along}

    def plane_peer(d):
        k = rem(plane + d, NA)
        return {"cross": rem(k, NC), "along": z * 2 + lax.div(k, NC)}

    def z_peer(d, y=ylo):
        return {"cross": cross, "along": rem(z + d, NZ) * 2 + y}

    def signal(sem, peer):
        pl.semaphore_signal(sem, inc=1, device_id=peer, device_id_type=MESH)

    barrier = pltpu.get_barrier_semaphore()
    for d in (1, NZ - 1):
        for y in range(2):
            signal(barrier, z_peer(d, y))

    @pl.loop(1, NA)
    def _(d):
        signal(barrier, plane_peer(d))

    def tell(k):
        for d in (2**k, NZ - 2**k):
            signal(near.at[k], z_peer(d))

    def hear(k):
        pl.semaphore_wait(near.at[k], 2)

    for copy in loads:
        copy.wait()

    lane = lax.broadcasted_iota(jnp.int32, (128, 128), 1)
    for b in range(2):
        rows = pl.ds(8 + 128 * b, 128)
        fields = [wid[rows].astype(F32)] + [fld[k, rows] for k in (1, 2, 0, 3)]
        slab = jnp.zeros((128, 128), F32)
        for k, f in enumerate(fields):
            x = jnp.where(lane < 64, f[:, :128], f[:, 128:])
            x = pltpu.roll(x, 16 * k + 8, 1)
            slab = jnp.where((lane >= 16 * k) & (lane < 16 * k + 16), x, slab)
        tsl[:, :, :, pl.ds(128 * b, 128)] = slab.T.reshape(8, 2, 8, 128)

    @pl.when(along == NA - 1)
    def _():
        tsl[0, 0] = jnp.zeros((8, 256), F32)
        tsl[3, 0] = jnp.zeros((8, 256), F32)

    @pl.when(along == 0)
    def _():
        tsl[0, 1] = jnp.zeros((8, 256), F32)
        tsl[3, 1] = jnp.zeros((8, 256), F32)

    asl[5:8] = jnp.zeros((3, 2, 8, 256), F32)
    for side in range(2):
        bsl[side, 3:8] = jnp.zeros((5, 2, 8, 128), F32)

    pl.semaphore_wait(barrier, NA - 1 + 4)
    tell(0)

    halo = []
    for k in range(5):
        ref = wid if k == 4 else fld.at[k]
        for side, (src, dst, step) in enumerate(((256, 0, 1), (8, 264, NC - 1))):
            halo.append(
                pltpu.make_async_remote_copy(
                    src_ref=ref.at[pl.ds(src, 8)],
                    dst_ref=ref.at[pl.ds(dst, 8)],
                    send_sem=row_s.at[2 * k + side],
                    recv_sem=row_r.at[2 * k + side],
                    device_id=cross_peer(step),
                    device_id_type=MESH,
                )
            )
    cols = []
    for side, step in enumerate((1, NA - 1)):
        cols.append(
            pltpu.make_async_remote_copy(
                src_ref=tsl.at[pl.ds(0, 5), side],
                dst_ref=asl.at[pl.ds(0, 5), side],
                send_sem=col_s.at[side],
                recv_sem=col_r.at[side],
                device_id=along_peer(step),
                device_id_type=MESH,
            )
        )
    for copy in cols + halo:
        copy.start()

    for copy in mats:
        copy.wait()
    for src, dst in ((om, omh), (th, thh), (lm, lmh), (rm, rmh)):
        hi, lo = split(src[...])
        dst[0] = hi
        dst[1] = lo

    for copy in cols:
        copy.wait_recv()

    corners = []
    for side, step in enumerate((1, NC - 1)):
        corners.append(
            pltpu.make_async_remote_copy(
                src_ref=asl.at[pl.ds(0, 3), :, :, pl.ds(128 * (1 - side), 128)],
                dst_ref=bsl.at[side, pl.ds(0, 3)],
                send_sem=cor_s.at[side],
                recv_sem=cor_r.at[side],
                device_id=cross_peer(step),
                device_id_type=MESH,
            )
        )
    for copy in corners:
        copy.start()

    for b in range(2):
        xs[pl.ds(128 * b, 128)] = asl[:, :, :, pl.ds(128 * b, 128)].reshape(128, 128).T

    hear(0)
    tell(1)
    for copy in halo:
        copy.wait_recv()

    @pl.when(cross == 0)
    def _():
        fld[0, pl.ds(0, 8)] = jnp.zeros((8, 256), F32)
        wid[pl.ds(0, 8)] = jnp.zeros((8, 256), jnp.int32)

    @pl.when(cross == NC - 1)
    def _():
        fld[0, pl.ds(264, 8)] = jnp.zeros((8, 256), F32)
        wid[pl.ds(264, 8)] = jnp.zeros((8, 256), jnp.int32)

    def beside(x, k):
        return pltpu.roll(x, 128 - (16 * k + 8), 1)

    def sp_rows(r, n, lead):
        w = wid[pl.ds(r, n)].astype(F32)
        wp = w * fld[1, pl.ds(r, n)]
        c = fld[3, pl.ds(r, n)]
        e = fld[0, pl.ds(pl.multiple_of(r - lead, 8), n + 16)]
        de = d12(e, 0)[lead : lead + n]
        wpx[pl.ds(r, n)] = wp
        sph[pl.ds(r, n)] = 2.0 * wp - w * c * ALPHA * de - (0.02 / c) * wp

    @pl.loop(0, 256 // CH)
    def _(i):
        sp_rows(pl.multiple_of(8 + i * CH, 8), CH, 8)

    sp_rows(0, 8, 0)
    sp_rows(264, 8, 16)
    hear(1)
    tell(2)

    @pl.loop(0, 256 // CH)
    def _(i):
        r0 = pl.multiple_of(i * CH, 8)
        r = pl.multiple_of(8 + i * CH, 8)
        own = pl.ds(r, CH)
        x = xs[pl.ds(r0, CH)]
        wt = wid[own].astype(F32)
        e0 = fld[0, own]
        w = jnp.concatenate([wt, beside(x, 0)], axis=1)
        q = jnp.concatenate([fld[2, own], beside(x, 2)], axis=1)
        e = jnp.concatenate([e0, beside(x, 3)], axis=1)
        c = jnp.concatenate([fld[3, own], beside(x, 4)], axis=1)
        wq = w * q
        sq = 2.0 * wq - w * c * ALPHA * d12(e, 1) - (0.02 / c) * wq
        dy = d12(sq, 1)[:, :256]
        s = sph[pl.ds(pl.multiple_of(r - 8, 8), CH + 16)]
        dx = d12(s, 0)[8 : 8 + CH]
        en = e0 - (0.5 * ALPHA) * wt * (dx + dy)
        sv[pl.ds(r0, CH)] = en
        hi, lo = split(en)
        shl[0, pl.ds(r0, CH)] = hi
        shl[1, pl.ds(r0, CH)] = lo

    def send(n, peer, src, dst, phase, s_sem, r_sem):
        def one(d):
            pltpu.make_async_remote_copy(
                src_ref=src(d),
                dst_ref=dst(d),
                send_sem=s_sem.at[phase],
                recv_sem=r_sem.at[phase],
                device_id=peer(d),
                device_id_type=MESH,
            ).start()

        one(n // 2)

        @pl.loop(1, n // 2)
        def _(s):
            one(n // 2 - s)
            one(n // 2 + s)

    def await_recv(ref, sem):
        pltpu.make_async_copy(ref, ref, sem).wait()

    surf = (shl[0], shl[1])
    tr = dot3(surf, (rmh[0], rmh[1]))
    kpart[...] = dot3((lmh[0], lmh[1]), split(tr)).reshape(NA, 8, 256)
    send(NA, plane_peer, lambda d: kpart.at[rem(plane + d, NA)], lambda d: krec.at[d], 1, rs_s, rs_r)
    rpart[...] = dot3(surf, (omh[0], omh[1])).reshape(NA, 8, 128)
    hear(2)
    send(NA, along_peer, lambda d: rpart.at[rem(along + d, NA)], lambda d: rrec.at[d], 0, rs_s, rs_r)
    cpart[...] = dot3((thh[0], thh[1]), surf).reshape(NC, 8, 256)
    send(NC, cross_peer, lambda d: cpart.at[rem(cross + d, NC)], lambda d: crec.at[d], 2, rs_s, rs_r)

    for copy in corners:
        copy.wait_recv()

    @pl.when(cross == 0)
    def _():
        bsl[0] = jnp.zeros((8, 2, 8, 128), F32)

    @pl.when(cross == NC - 1)
    def _():
        bsl[1] = jnp.zeros((8, 2, 8, 128), F32)

    for side in range(2):
        t = bsl[side, pl.ds(0, 8)].reshape(128, 128).T
        xb[pl.ds(8 * side, 8)] = t[120:128] if side == 0 else t[0:8]

    def e1_rows(r, n, x, lead):
        w = wid[pl.ds(r, n)].astype(F32)
        wq = jnp.concatenate(
            [w * fld[2, pl.ds(r, n)], beside(x, 0) * beside(x, 2)], axis=1
        )
        wp = wpx[pl.ds(pl.multiple_of(r - lead, 8), n + 16)]
        dx = d12(wp, 0)[lead : lead + n]
        dy = d12(wq, 1)[:, :256]
        e = fld[0, pl.ds(r, n)]
        return e + (e - ALPHA * w * (dx + dy))

    @pl.loop(0, 256 // CH)
    def _(i):
        r = pl.multiple_of(8 + i * CH, 8)
        e1x[pl.ds(r, CH)] = e1_rows(r, CH, xs[pl.ds(pl.multiple_of(i * CH, 8), CH)], 8)

    e1x[pl.ds(0, 8)] = e1_rows(0, 8, xb[pl.ds(0, 8)], 0)
    e1x[pl.ds(264, 8)] = e1_rows(264, 8, xb[pl.ds(8, 8)], 16)

    xb[pl.ds(16, 256)] = xs[...]

    @pl.loop(0, 256 // CH)
    def _(i):
        r0 = pl.multiple_of(i * CH, 8)
        r = pl.multiple_of(8 + i * CH, 8)
        own = pl.ds(r, CH)
        x = xs[pl.ds(r0, CH)]
        w = wid[own].astype(F32)
        c = fld[3, own]
        p, q = fld[1, own], fld[2, own]
        wc = w * c * ALPHA
        fr = w * (0.02 / c)
        p1 = p - wc * d12(fld[0, pl.ds(r0, CH + 16)], 0)[8 : 8 + CH] - fr * p
        ee = e1x[pl.ds(r0, CH + 16)]
        dx = d12(ee, 0)[8 : 8 + CH]
        pv[pl.ds(r0, CH)] = p - 0.5 * (wc * dx + fr * (p + p1))

        hb = jnp.concatenate(
            [
                jnp.where(i == 0, xb[pl.ds(0, 8)], xb[pl.ds(pl.multiple_of(jnp.maximum(r0 + 8, 8), 8), 8)]),
                x,
                jnp.where(
                    i == 256 // CH - 1,
                    xb[pl.ds(8, 8)],
                    xb[pl.ds(pl.multiple_of(jnp.minimum(r0 + 16 + CH, 264), 8), 8)],
                ),
            ],
            axis=0,
        )
        wpb = beside(hb, 0) * beside(hb, 1)
        dxb = d12(wpb, 0)[8 : 8 + CH]
        wb = beside(x, 0)
        wq = jnp.concatenate([w * q, wb * beside(x, 2)], axis=1)
        dyb = d12(wq, 1)[:, 256:]
        eb = beside(x, 3)
        e1b = eb + (eb - ALPHA * wb * (dxb + dyb))
        e = jnp.concatenate([fld[0, own], eb], axis=1)
        q1 = q - wc * d12(e, 1)[:, :256] - fr * q
        dy = d12(jnp.concatenate([e1x[own], e1b], axis=1), 1)[:, :256]
        qv[pl.ds(r0, CH)] = q - 0.5 * (wc * dy + fr * (q + q1))

    await_recv(krec.at[pl.ds(1, NA - 1)], rs_r.at[1])
    krec[0] = kpart[plane]
    ksum[...] = jnp.sum(krec[...], axis=0)
    send(NZ, z_peer, lambda d: ksum, lambda d: zrec.at[d], 3, rs_s, rs_r)

    await_recv(crec.at[pl.ds(1, NC - 1)], rs_r.at[2])
    crec[0] = cpart[cross]
    csum[pl.ds(pl.multiple_of(8 * cross, 8), 8)] = jnp.sum(crec[...], axis=0)
    mine = pl.ds(pl.multiple_of(8 * cross, 8), 8)
    send(NC, cross_peer, lambda d: csum.at[mine], lambda d: csum.at[mine], 2, ag_s, ag_r)

    await_recv(rrec.at[pl.ds(1, NA - 1)], rs_r.at[0])
    rrec[0] = rpart[along]
    rsum[z, ylo] = jnp.sum(rrec[...], axis=0)
    own_r = rsum.at[z, ylo]
    send(NZ, z_peer, lambda d: own_r, lambda d: own_r, 0, ag_s, ag_r)

    await_recv(zrec.at[pl.ds(1, NZ - 1)], rs_r.at[3])
    zrec[0] = ksum[...]
    total = zrec[z]
    for k in range(1, NZ):
        total = total + zrec[rem(z - k + NZ, NZ)]
    own_k = pl.ds(pl.multiple_of(8 * plane, 8), 8)
    zsum[own_k] = total
    send(NA, plane_peer, lambda d: zsum.at[own_k], lambda d: zsum.at[own_k], 1, ag_s, ag_r)

    await_recv(csum.at[pl.ds(0, 120)], ag_r.at[2])
    await_recv(rsum.at[pl.ds(0, NZ - 1), 0], ag_r.at[0])
    pair = pltpu.make_async_remote_copy(
        src_ref=rsum.at[:, ylo],
        dst_ref=rsum.at[:, ylo],
        send_sem=ag_s.at[3],
        recv_sem=ag_r.at[3],
        device_id={"cross": cross, "along": z * 2 + 1 - ylo},
        device_id_type=MESH,
    )
    pair.start()
    await_recv(zsum.at[pl.ds(0, 248)], ag_r.at[1])
    pair.wait_recv()

    for copy in halo + cols + corners + [pair]:
        copy.wait_send()
    await_recv(rrec.at[pl.ds(1, NA - 1)], rs_s.at[0])
    await_recv(krec.at[pl.ds(1, NA - 1)], rs_s.at[1])
    await_recv(crec.at[pl.ds(1, NC - 1)], rs_s.at[2])
    await_recv(zrec.at[pl.ds(1, NZ - 1)], rs_s.at[3])
    await_recv(rsum.at[pl.ds(0, NZ - 1), 0], ag_s.at[0])
    await_recv(zsum.at[pl.ds(0, 248)], ag_s.at[1])
    await_recv(csum.at[pl.ds(0, 120)], ag_s.at[2])


def write_out(*refs):
    ins, outs, sem = refs[:6], refs[6:12], refs[12]
    copies = [pltpu.make_async_copy(a, b, sem.at[k]) for k, (a, b) in enumerate(zip(ins, outs))]
    for copy in copies:
        copy.start()
    for copy in copies:
        copy.wait()


def body(*args):
    vm = pltpu.VMEM
    dma = pltpu.SemaphoreType.DMA
    sds = jax.ShapeDtypeStruct
    held = pl.pallas_call(
        kernel,
        out_shape=(
            sds((256, 256), F32),
            sds((256, 256), F32),
            sds((256, 256), F32),
            sds((NZ, 2, 8, 128), F32),
            sds((128, 256), F32),
            sds((256, 256), F32),
        ),
        in_specs=[pl.BlockSpec(memory_space=pl.ANY)] * 9,
        out_specs=[pl.BlockSpec(memory_space=pltpu.VMEM)] * 6,
        scratch_shapes=[
            vm((4, 272, 256), F32),
            vm((272, 256), jnp.int32),
            vm((8, 2, 8, 256), F32),
            vm((8, 2, 8, 256), F32),
            vm((2, 8, 2, 8, 128), F32),
            vm((256, 128), F32),
            vm((272, 128), F32),
            vm((272, 256), F32),
            vm((272, 256), F32),
            vm((272, 256), F32),
            vm((2, 256, 256), BF16),
            vm((256, 128), F32),
            vm((128, 256), F32),
            vm((256, 256), F32),
            vm((256, 256), F32),
            vm((2, 256, 128), BF16),
            vm((2, 128, 256), BF16),
            vm((2, 256, 256), BF16),
            vm((2, 256, 256), BF16),
            vm((NA, 8, 128), F32),
            vm((NC, 8, 256), F32),
            vm((NA, 8, 256), F32),
            vm((NA, 8, 128), F32),
            vm((NC, 8, 256), F32),
            vm((NA, 8, 256), F32),
            vm((NZ, 8, 256), F32),
            vm((8, 256), F32),
            dma((9,)),
            dma((10,)),
            dma((10,)),
            dma((2,)),
            dma((2,)),
            dma((2,)),
            dma((2,)),
            dma((4,)),
            dma((4,)),
            dma((4,)),
            dma((4,)),
            pltpu.SemaphoreType.REGULAR((3,)),
        ],
        compiler_params=pltpu.CompilerParams(collective_id=0, has_side_effects=True, vmem_limit_bytes=16 << 20),
    )(*[pltpu.with_memory_space_constraint(a, pltpu.HBM) for a in args])
    held = held[:3] + (held[3].reshape(256, 128),) + held[4:]
    return pl.pallas_call(
        write_out,
        out_shape=tuple(sds(x.shape, F32) for x in held),
        in_specs=[pl.BlockSpec(memory_space=pltpu.VMEM)] * 6,
        out_specs=[pl.BlockSpec(memory_space=pl.ANY)] * 6,
        scratch_shapes=[dma((6,))],
        compiler_params=pltpu.CompilerParams(vmem_limit_bytes=8 << 20),
    )(*held)


def solution(mesh):
    return jax.shard_map(
        body,
        mesh=mesh,
        in_specs=(
            P("cross", "along"),
            P("cross", "along"),
            P("cross", "along"),
            P("cross", "along"),
            P("cross", "along"),
            P("along", None),
            P(None, "cross"),
            P(None, "cross"),
            P("along", None),
        ),
        out_specs=(
            P("cross", "along"),
            P("cross", "along"),
            P("cross", "along"),
            P("cross", None),
            P(None, "along"),
            P(),
        ),
        check_vma=False,
    )
```

```python
import functools

import jax
import jax.numpy as jnp
from jax import lax
from jax.experimental import pallas as pl
from jax.experimental.pallas import tpu as pltpu
from jax.sharding import PartitionSpec as P

MESH = pl.DeviceIdType.MESH
F32 = jnp.float32
BF16 = jnp.bfloat16
NC = 16
NA = 32
NZ = 16
ALPHA = 0.25 / 12.0
CH = 32
CHS = 128
CHF = 64
PLANE = sorted(
    ((dy, dx, dc) for dy in range(4) for dx in range(4) for dc in range(2) if (dy, dx, dc) != (0, 0, 0)),
    key=lambda d: -(min(d[0], 4 - d[0]) + min(d[1], 4 - d[1])),
)


def split(x):
    hi = x.astype(BF16)
    return hi, (x - hi.astype(F32)).astype(BF16)


def dot3(a, b):
    dot = functools.partial(jnp.dot, preferred_element_type=F32)
    (ah, al), (bh, bl) = a, b
    return dot(ah, bh) + (dot(ah, bl) + dot(al, bh))


def d12(f, axis):
    n = f.shape[axis]
    up1, dn1 = pltpu.roll(f, n - 1, axis), pltpu.roll(f, 1, axis)
    up2, dn2 = pltpu.roll(f, n - 2, axis), pltpu.roll(f, 2, axis)
    return 8.0 * (up1 - dn1) - (up2 - dn2)


def kernel(
    e_in, p_in, q_in, c_in, w_in, om_in, th_in, l_in, r_in,
    sv, pv, qv, rsum, csum, zsum,
    fld, wid, hal, haw, tsl, asl, bsl, xs, xb, sph, wpx, e1x, wcs, frs, zx, zy, edg, shl,
    om, th, lm, rm, omh, thh, lmh, rmh,
    rpart, cpart, kpart, rrec, crec, krec, zrec, ksum,
    in_sem, row_s, row_r, col_s, col_r, cor_s, cor_r,
    rs_s, rs_r, ag_s, ag_r, near,
):
    cross = lax.axis_index("cross")
    along = lax.axis_index("along")
    z, ylo = along // 2, along % 2
    yhi, x_at, core = cross // 8, cross // 2 % 4, cross % 2
    y_at = yhi * 2 + ylo
    plane = y_at * 8 + x_at * 2 + core

    loads = [
        pltpu.make_async_copy(src, fld.at[k, pl.ds(8, 256)], in_sem.at[k])
        for k, src in enumerate((e_in, p_in, q_in, c_in))
    ]
    loads.append(pltpu.make_async_copy(w_in, wid.at[pl.ds(8, 256)], in_sem.at[4]))
    for copy in loads:
        copy.start()
    mats = [
        pltpu.make_async_copy(src, dst, in_sem.at[5 + k])
        for k, (src, dst) in enumerate(((om_in, om), (th_in, th), (l_in, lm), (r_in, rm)))
    ]
    for copy in mats:
        copy.start()

    rem = lax.rem

    def along_peer(d):
        return {"cross": cross, "along": rem(along + d, NA)}

    def cross_peer(d):
        return {"cross": rem(cross + d, NC), "along": along}

    def plane_at(dy, dx, dc):
        return rem(y_at + dy, 4), rem(x_at + dx, 4), rem(core + dc, 2)

    def plane_peer(dy, dx, dc):
        y, x, c = plane_at(dy, dx, dc)
        return {"cross": lax.div(y, 2) * 8 + x * 2 + c, "along": z * 2 + rem(y, 2)}

    def z_peer(d, y=ylo):
        return {"cross": cross, "along": rem(z + d, NZ) * 2 + y}

    def signal(sem, peer):
        pl.semaphore_signal(sem, inc=1, device_id=peer, device_id_type=MESH)

    barrier = pltpu.get_barrier_semaphore()
    for d in (1, NZ - 1):
        for y in range(2):
            signal(barrier, z_peer(d, y))

    for d in PLANE:
        signal(barrier, plane_peer(*d))

    def tell(k):
        for d in (2**k, NZ - 2**k):
            signal(near.at[k], z_peer(d))

    def hear(k):
        pl.semaphore_wait(near.at[k], 2)

    for copy in loads:
        copy.wait()

    lane = lax.broadcasted_iota(jnp.int32, (128, 128), 1)
    for b in range(2):
        rows = pl.ds(8 + 128 * b, 128)
        fields = [wid[rows].astype(F32)] + [fld[k, rows] for k in (1, 2, 0, 3)]
        slab = jnp.zeros((128, 128), F32)
        for k, f in enumerate(fields):
            x = pltpu.roll(jnp.where(lane < 64, f[:, :128], f[:, 128:]), 8 * (k + 1), 1)
            slab = jnp.where((lane >= 8 * k + 4) & (lane < 8 * k + 12), x, slab)
        tsl[:, :, pl.ds(128 * b, 128)] = slab.T.reshape(16, 8, 128)

    @pl.when(along == 0)
    def _():
        asl[7:11, 4:8] = jnp.zeros((4, 4, 256), F32)
        asl[11, 4:8] = jnp.ones((4, 256), F32)

    @pl.when(along == NA - 1)
    def _():
        asl[0:4, 0:4] = jnp.zeros((4, 4, 256), F32)
        asl[4, 0:4] = jnp.ones((4, 256), F32)

    for side, edge in enumerate((0, NC - 1)):

        @pl.when(cross == edge)
        def _():
            hal[0:3, side] = jnp.zeros((3, 8, 256), F32)
            hal[3, side] = jnp.ones((8, 256), F32)
            haw[side] = jnp.zeros((8, 256), jnp.int32)
            bsl[side] = jnp.zeros((16, 8, 128), F32)

    pl.semaphore_wait(barrier, NA - 1 + 4)
    tell(0)

    def remote(src, dst, sems, k, peer):
        return pltpu.make_async_remote_copy(
            src_ref=src,
            dst_ref=dst,
            send_sem=sems[0].at[k],
            recv_sem=sems[1].at[k],
            device_id=peer,
            device_id_type=MESH,
        )

    cols = [
        remote(tsl.at[pl.ds(0, 5), pl.ds(4, 4)], asl.at[pl.ds(7, 5), pl.ds(4, 4)], (col_s, col_r), 0, along_peer(1)),
        remote(tsl.at[pl.ds(1, 5), pl.ds(0, 4)], asl.at[pl.ds(0, 5), pl.ds(0, 4)], (col_s, col_r), 1, along_peer(NA - 1)),
    ]
    halo = [[], []]
    for side, (src, dst, step) in enumerate(((260, 4, 1), (8, 0, NC - 1))):
        for k in (0, 1, 4, 3, 2):
            ref, to = (wid, haw) if k == 4 else (fld.at[k], hal.at[k])
            halo[side].append(
                remote(
                    ref.at[pl.ds(src, 4)], to.at[side, pl.ds(dst, 4)], (row_s, row_r), 2 * k + side, cross_peer(step)
                )
            )
    goes = (cross < NC - 1, cross > 0)
    comes = (cross > 0, cross < NC - 1)
    goes_a = (along < NA - 1, along > 0)
    comes_a = (along > 0, along < NA - 1)

    def only(cond, *acts):
        @pl.when(cond)
        def _():
            for act in acts:
                act()

    for side in range(2):
        only(goes[side], *[copy.start for copy in halo[side]])
    for side in range(2):
        only(goes_a[side], cols[side].start)

    for copy in mats:
        copy.wait()
    for src, dst in ((om, omh), (th, thh), (lm, lmh), (rm, rmh)):
        hi, lo = split(src[...])
        dst[0] = hi
        dst[1] = lo

    def coefficients(w, c):
        return w * c * ALPHA, w * (0.02 / c)

    zero8 = jnp.zeros((8, 256), F32)
    for ref in (fld.at[0], sph):
        ref[pl.ds(0, 8)] = zero8
        ref[pl.ds(264, 8)] = zero8


    def edges(f):
        lanes = lax.broadcasted_iota(jnp.int32, (CH, 128), 1)
        return jnp.where(lanes >= 96, f[:, 128:], pltpu.roll(f[:, :128], 64, 1))

    def inside(i):
        r0 = pl.multiple_of(i * CH, 8)
        here = pl.ds(r0, CH)
        own = pl.ds(pl.multiple_of(8 + i * CH, 8), CH)
        w = wid[own].astype(F32)
        e, p, q, c = (fld[k, own] for k in range(4))
        wc, fr = coefficients(w, c)
        wcs[here] = wc
        frs[here] = fr
        wp, wq = w * p, w * q
        wpx[own] = wp
        de = d12(fld[0, pl.ds(r0, CH + 16)], 0)[8 : 8 + CH]
        sph[own] = 2.0 * wp - wc * de - fr * wp
        sq = 2.0 * wq - wc * d12(e, 1) - fr * wq
        zy[here] = d12(sq, 1)
        for k, f in enumerate((w, wq, e, wc, fr)):
            edg[k, here] = edges(f)

    pl.loop(0, 128 // CH)(inside)
    hear(0)
    tell(1)
    pl.loop(128 // CH, 256 // CH)(inside)

    @pl.loop(0, 256 // CH)
    def _(i):
        r0 = pl.multiple_of(i * CH, 8)
        zx[pl.ds(r0, CH)] = d12(sph[pl.ds(r0, CH + 16)], 0)[8 : 8 + CH]

    for side in range(2):
        only(comes_a[side], cols[side].wait_recv)
    hear(1)
    tell(2)

    corners = []
    for side, step in enumerate((1, NC - 1)):
        part = pl.ds(128 * (1 - side), 128)
        corners.append(
            [
                remote(
                    asl.at[pl.ds(tile, 3), pl.ds(row, 4), part],
                    bsl.at[side, pl.ds(tile, 3), pl.ds(row, 4)],
                    (cor_s, cor_r),
                    2 * side + k,
                    cross_peer(step),
                )
                for k, (tile, row) in enumerate(((0, 0), (7, 4)))
            ]
        )
    for side in range(2):
        only(goes[side], *[copy.start for copy in corners[side]])

    for b in range(2):
        xs[pl.ds(128 * b, 128)] = asl[:, :, pl.ds(128 * b, 128)].reshape(128, 128).T

    def beside(x, k):
        return pltpu.roll(x, 128 - 8 * k, 1) if k else x

    for side in range(2):
        only(comes[side], *[copy.wait_recv for copy in halo[side]])
    for side, at in enumerate((0, 264)):
        for k in range(4):
            fld[k, pl.ds(at, 8)] = hal[k, side]
        wid[pl.ds(at, 8)] = haw[side]

    for at, off in ((0, 0), (256, 8)):
        rows = pl.ds(at, 16)
        w = wid[rows].astype(F32)
        wc, fr = coefficients(w, fld[3, rows])
        wp = w * fld[1, rows]
        wpx[rows] = wp
        de = d12(fld[0, pl.ds(at - off, 24)], 0)[off : off + 16]
        sph[rows] = 2.0 * wp - wc * de - fr * wp
    zx[pl.ds(0, 8)] = d12(sph[pl.ds(0, 24)], 0)[8:16]
    zx[pl.ds(248, 8)] = d12(sph[pl.ds(248, 24)], 0)[8:16]

    @pl.loop(0, 256 // CHS)
    def _(i):
        here = pl.ds(pl.multiple_of(i * CHS, 8), CHS)
        own = pl.ds(pl.multiple_of(8 + i * CHS, 8), CHS)
        x = xs[here]
        lanes = lax.broadcasted_iota(jnp.int32, (CHS, 128), 1)
        w = beside(x, 0)
        wc, fr = coefficients(w, beside(x, 4))
        w, wq, e, wc, fr = (
            jnp.where(lanes < 64, new, edg[k, here])
            for k, new in enumerate((w, w * beside(x, 2), beside(x, 3), wc, fr))
        )
        dy = d12(2.0 * wq - wc * d12(e, 1) - fr * wq, 1)
        z_y = zy[here]
        z_y = jnp.concatenate(
            [
                jnp.where(lanes < 8, pltpu.roll(dy, 64, 1), z_y[:, :128]),
                jnp.where(lanes >= 120, dy, z_y[:, 128:]),
            ],
            axis=1,
        )
        en = fld[0, own] - (0.5 * ALPHA) * wid[own].astype(F32) * (zx[here] + z_y)
        sv[here] = en
        hi, lo = split(en)
        shl[0, here] = hi
        shl[1, here] = lo

    def send(n, peer, src, dst, phase, s_sem, r_sem):
        def one(d):
            pltpu.make_async_remote_copy(
                src_ref=src(d),
                dst_ref=dst(d),
                send_sem=s_sem.at[phase],
                recv_sem=r_sem.at[phase],
                device_id=peer(*d) if peer is plane_peer else peer(d),
                device_id_type=MESH,
            ).start()

        if peer is plane_peer:
            for d in PLANE:
                one(d)
            return
        one(n // 2)

        @pl.loop(1, n // 2)
        def _(s):
            one(n // 2 - s)
            one(n // 2 + s)

    def await_recv(ref, sem):
        pltpu.make_async_copy(ref, ref, sem).wait()

    def place(y, x, c):
        return y * 8 + x * 2 + c

    surf = (shl[0], shl[1])
    tr = dot3(surf, (rmh[0], rmh[1]))
    kpart[...] = dot3((lmh[0], lmh[1]), split(tr)).reshape(NA, 8, 256)
    send(NA, plane_peer, lambda d: kpart.at[place(*plane_at(*d))], lambda d: krec.at[place(*d)], 1, rs_s, rs_r)
    rpart[...] = dot3(surf, (omh[0], omh[1])).reshape(NA, 8, 128)
    cpart[...] = dot3((thh[0], thh[1]), surf).reshape(NC, 8, 256)
    hear(2)
    send(NA, along_peer, lambda d: rpart.at[rem(along + d, NA)], lambda d: rrec.at[d], 0, rs_s, rs_r)

    for side in range(2):
        only(comes[side], *[copy.wait_recv for copy in corners[side]])
    for side in range(2):
        t = bsl[side].reshape(128, 128).T
        xb[pl.ds(8 * side, 8)] = t[120:128] if side == 0 else t[0:8]

    def ring(x):
        lane = lax.broadcasted_iota(jnp.int32, x.shape, 1)
        return jnp.where(lane < 32, x, pltpu.roll(x, 64, 1))

    def e1_rows(r, n, x, lead):
        w = wid[pl.ds(r, n)].astype(F32)
        wq = jnp.concatenate([w * fld[2, pl.ds(r, n)], ring(beside(x, 0) * beside(x, 2))], axis=1)
        wp = wpx[pl.ds(pl.multiple_of(r - lead, 8), n + 16)]
        dx = d12(wp, 0)[lead : lead + n]
        dy = d12(wq, 1)[:, :256]
        e = fld[0, pl.ds(r, n)]
        return e + (e - ALPHA * w * (dx + dy))

    @pl.loop(0, 256 // CHF)
    def _(i):
        r = pl.multiple_of(8 + i * CHF, 8)
        e1x[pl.ds(r, CHF)] = e1_rows(r, CHF, xs[pl.ds(pl.multiple_of(i * CHF, 8), CHF)], 8)

    e1x[pl.ds(0, 8)] = e1_rows(0, 8, xb[pl.ds(0, 8)], 0)
    e1x[pl.ds(264, 8)] = e1_rows(264, 8, xb[pl.ds(8, 8)], 16)

    send(NC, cross_peer, lambda d: cpart.at[rem(cross + d, NC)], lambda d: crec.at[d], 2, rs_s, rs_r)

    await_recv(krec.at[pl.ds(1, NA - 1)], rs_r.at[1])
    krec[0] = kpart[plane]
    ksum[...] = jnp.sum(krec[...], axis=0)
    send(NZ, z_peer, lambda d: ksum, lambda d: zrec.at[d], 3, rs_s, rs_r)

    xb[pl.ds(16, 256)] = xs[...]

    @pl.loop(0, 256 // CHF)
    def _(i):
        r0 = pl.multiple_of(i * CHF, 8)
        r = pl.multiple_of(8 + i * CHF, 8)
        own = pl.ds(r, CHF)
        x = xs[pl.ds(r0, CHF)]
        w = wid[own].astype(F32)
        p, q = fld[1, own], fld[2, own]
        wc, fr = wcs[pl.ds(r0, CHF)], frs[pl.ds(r0, CHF)]
        p1 = p - wc * d12(fld[0, pl.ds(r0, CHF + 16)], 0)[8 : 8 + CHF] - fr * p
        ee = e1x[pl.ds(r0, CHF + 16)]
        dx = d12(ee, 0)[8 : 8 + CHF]
        pv[pl.ds(r0, CHF)] = p - 0.5 * (wc * dx + fr * (p + p1))

        hb = jnp.concatenate(
            [
                jnp.where(i == 0, xb[pl.ds(0, 8)], xb[pl.ds(pl.multiple_of(jnp.maximum(r0 + 8, 8), 8), 8)]),
                x,
                jnp.where(
                    i == 256 // CHF - 1,
                    xb[pl.ds(8, 8)],
                    xb[pl.ds(pl.multiple_of(jnp.minimum(r0 + 16 + CHF, 264), 8), 8)],
                ),
            ],
            axis=0,
        )
        wpb = ring(beside(hb, 0) * beside(hb, 1))
        dxb = d12(wpb, 0)[8 : 8 + CHF]
        wb = ring(beside(x, 0))
        wq = jnp.concatenate([w * q, ring(beside(x, 0) * beside(x, 2))], axis=1)
        dyb = d12(wq, 1)[:, 256:]
        eb = ring(beside(x, 3))
        e1b = eb + (eb - ALPHA * wb * (dxb + dyb))
        e = jnp.concatenate([fld[0, own], eb], axis=1)
        q1 = q - wc * d12(e, 1)[:, :256] - fr * q
        dy = d12(jnp.concatenate([e1x[own], e1b], axis=1), 1)[:, :256]
        qv[pl.ds(r0, CHF)] = q - 0.5 * (wc * dy + fr * (q + q1))

    await_recv(rrec.at[pl.ds(1, NA - 1)], rs_r.at[0])
    rrec[0] = rpart[along]
    rsum[z, ylo] = jnp.sum(rrec[...], axis=0)
    own_r = rsum.at[z, ylo]
    send(NZ, z_peer, lambda d: own_r, lambda d: own_r, 0, ag_s, ag_r)

    await_recv(crec.at[pl.ds(1, NC - 1)], rs_r.at[2])
    crec[0] = cpart[cross]
    csum[pl.ds(pl.multiple_of(8 * cross, 8), 8)] = jnp.sum(crec[...], axis=0)
    mine = pl.ds(pl.multiple_of(8 * cross, 8), 8)
    send(NC, cross_peer, lambda d: csum.at[mine], lambda d: csum.at[mine], 2, ag_s, ag_r)

    await_recv(zrec.at[pl.ds(1, NZ - 1)], rs_r.at[3])
    zrec[0] = ksum[...]
    total = zrec[z]
    for k in range(1, NZ):
        total = total + zrec[rem(z - k + NZ, NZ)]
    own_k = pl.ds(pl.multiple_of(8 * plane, 8), 8)
    zsum[own_k] = total
    send(NA, plane_peer, lambda d: zsum.at[own_k], lambda d: zsum.at[own_k], 1, ag_s, ag_r)

    await_recv(csum.at[pl.ds(0, 120)], ag_r.at[2])
    await_recv(rsum.at[pl.ds(0, NZ - 1), 0], ag_r.at[0])
    pair = pltpu.make_async_remote_copy(
        src_ref=rsum.at[:, ylo],
        dst_ref=rsum.at[:, ylo],
        send_sem=ag_s.at[3],
        recv_sem=ag_r.at[3],
        device_id={"cross": cross, "along": z * 2 + 1 - ylo},
        device_id_type=MESH,
    )
    pair.start()
    await_recv(zsum.at[pl.ds(0, 248)], ag_r.at[1])
    pair.wait_recv()

    for side in range(2):
        only(goes[side], *[copy.wait_send for copy in halo[side] + corners[side]])
        only(goes_a[side], cols[side].wait_send)
    pair.wait_send()
    await_recv(rrec.at[pl.ds(1, NA - 1)], rs_s.at[0])
    await_recv(krec.at[pl.ds(1, NA - 1)], rs_s.at[1])
    await_recv(crec.at[pl.ds(1, NC - 1)], rs_s.at[2])
    await_recv(zrec.at[pl.ds(1, NZ - 1)], rs_s.at[3])
    await_recv(rsum.at[pl.ds(0, NZ - 1), 0], ag_s.at[0])
    await_recv(zsum.at[pl.ds(0, 248)], ag_s.at[1])
    await_recv(csum.at[pl.ds(0, 120)], ag_s.at[2])


def write_out(*refs):
    ins, outs, sem = refs[:6], refs[6:12], refs[12]
    copies = [pltpu.make_async_copy(a, b, sem.at[k]) for k, (a, b) in enumerate(zip(ins, outs))]
    for copy in copies:
        copy.start()
    for copy in copies:
        copy.wait()


def body(*args):
    vm = pltpu.VMEM
    dma = pltpu.SemaphoreType.DMA
    sds = jax.ShapeDtypeStruct
    held = pl.pallas_call(
        kernel,
        out_shape=(
            sds((256, 256), F32),
            sds((256, 256), F32),
            sds((256, 256), F32),
            sds((NZ, 2, 8, 128), F32),
            sds((128, 256), F32),
            sds((256, 256), F32),
        ),
        in_specs=[pl.BlockSpec(memory_space=pl.ANY)] * 9,
        out_specs=[pl.BlockSpec(memory_space=pltpu.VMEM)] * 6,
        scratch_shapes=[
            vm((4, 272, 256), F32),
            vm((272, 256), jnp.int32),
            vm((4, 2, 8, 256), F32),
            vm((2, 8, 256), jnp.int32),
            vm((16, 8, 256), F32),
            vm((16, 8, 256), F32),
            vm((2, 16, 8, 128), F32),
            vm((256, 128), F32),
            vm((272, 128), F32),
            vm((272, 256), F32),
            vm((272, 256), F32),
            vm((272, 256), F32),
            vm((256, 256), F32),
            vm((256, 256), F32),
            vm((256, 256), F32),
            vm((256, 256), F32),
            vm((5, 256, 128), F32),
            vm((2, 256, 256), BF16),
            vm((256, 128), F32),
            vm((128, 256), F32),
            vm((256, 256), F32),
            vm((256, 256), F32),
            vm((2, 256, 128), BF16),
            vm((2, 128, 256), BF16),
            vm((2, 256, 256), BF16),
            vm((2, 256, 256), BF16),
            vm((NA, 8, 128), F32),
            vm((NC, 8, 256), F32),
            vm((NA, 8, 256), F32),
            vm((NA, 8, 128), F32),
            vm((NC, 8, 256), F32),
            vm((NA, 8, 256), F32),
            vm((NZ, 8, 256), F32),
            vm((8, 256), F32),
            dma((9,)),
            dma((10,)),
            dma((10,)),
            dma((2,)),
            dma((2,)),
            dma((4,)),
            dma((4,)),
            dma((4,)),
            dma((4,)),
            dma((4,)),
            dma((4,)),
            pltpu.SemaphoreType.REGULAR((3,)),
        ],
        compiler_params=pltpu.CompilerParams(collective_id=0, has_side_effects=True, vmem_limit_bytes=16 << 20),
    )(*[pltpu.with_memory_space_constraint(a, pltpu.HBM) for a in args])
    held = held[:3] + (held[3].reshape(256, 128),) + held[4:]
    return pl.pallas_call(
        write_out,
        out_shape=tuple(sds(x.shape, F32) for x in held),
        in_specs=[pl.BlockSpec(memory_space=pltpu.VMEM)] * 6,
        out_specs=[pl.BlockSpec(memory_space=pl.ANY)] * 6,
        scratch_shapes=[dma((6,))],
        compiler_params=pltpu.CompilerParams(vmem_limit_bytes=8 << 20),
    )(*held)


def solution(mesh):
    return jax.shard_map(
        body,
        mesh=mesh,
        in_specs=(
            P("cross", "along"),
            P("cross", "along"),
            P("cross", "along"),
            P("cross", "along"),
            P("cross", "along"),
            P("along", None),
            P(None, "cross"),
            P(None, "cross"),
            P("along", None),
        ),
        out_specs=(
            P("cross", "along"),
            P("cross", "along"),
            P("cross", "along"),
            P("cross", None),
            P(None, "along"),
            P(),
        ),
        check_vma=False,
    )
```

```python
import functools

import jax
import jax.numpy as jnp
from jax import lax
from jax.experimental import pallas as pl
from jax.experimental.pallas import tpu as pltpu
from jax.sharding import PartitionSpec as P

MESH = pl.DeviceIdType.MESH
F32 = jnp.float32
BF16 = jnp.bfloat16
NC = 16
NA = 32
NZ = 16
ALPHA = 0.25 / 12.0
CH = 64
CHS = 256
CHF = 64
PLANE = sorted(
    ((dy, dx, dc) for dy in range(4) for dx in range(4) for dc in range(2) if (dy, dx, dc) != (0, 0, 0)),
    key=lambda d: -(min(d[0], 4 - d[0]) + min(d[1], 4 - d[1])),
)

NEXT = [d for d in PLANE if min(d[0], 4 - d[0]) + min(d[1], 4 - d[1]) <= 2]


def split(x):
    hi = x.astype(BF16)
    return hi, (x - hi.astype(F32)).astype(BF16)


def dot3(a, b):
    dot = functools.partial(jnp.dot, preferred_element_type=F32)
    (ah, al), (bh, bl) = a, b
    return dot(ah, bh) + (dot(ah, bl) + dot(al, bh))


def d12(f, axis):
    n = f.shape[axis]
    up1, dn1 = pltpu.roll(f, n - 1, axis), pltpu.roll(f, 1, axis)
    up2, dn2 = pltpu.roll(f, n - 2, axis), pltpu.roll(f, 2, axis)
    return 8.0 * (up1 - dn1) - (up2 - dn2)


def kernel(
    e_in, p_in, q_in, c_in, w_in, om_in, th_in, l_in, r_in,
    sv, pv, qv, rsum, csum, zsum,
    fld, wid, hal, haw, tsl, asl, bsl, xs, xb, sph, wpx, e1x, wcs, frs, zx, zy, edg, shl,
    om, th, lm, rm, omh, thh, lmh, rmh,
    rpart, cpart, kpart, rrec, crec, krec, zrec, ksum,
    in_sem, row_s, row_r, col_s, col_r, cor_s, cor_r,
    rs_s, rs_r, ag_s, ag_r, near,
):
    cross = lax.axis_index("cross")
    along = lax.axis_index("along")
    z, ylo = along // 2, along % 2
    yhi, x_at, core = cross // 8, cross // 2 % 4, cross % 2
    y_at = yhi * 2 + ylo
    plane = y_at * 8 + x_at * 2 + core

    loads = [
        pltpu.make_async_copy(src, fld.at[k, pl.ds(8, 256)], in_sem.at[k])
        for k, src in enumerate((e_in, p_in, q_in, c_in))
    ]
    loads.append(pltpu.make_async_copy(w_in, wid.at[pl.ds(8, 256)], in_sem.at[4]))
    for copy in loads:
        copy.start()
    mats = [
        pltpu.make_async_copy(src, dst, in_sem.at[5 + k])
        for k, (src, dst) in enumerate(((om_in, om), (th_in, th), (l_in, lm), (r_in, rm)))
    ]
    for copy in mats:
        copy.start()

    rem = lax.rem

    def along_peer(d):
        return {"cross": cross, "along": rem(along + d, NA)}

    def cross_peer(d):
        return {"cross": rem(cross + d, NC), "along": along}

    def plane_at(dy, dx, dc):
        return rem(y_at + dy, 4), rem(x_at + dx, 4), rem(core + dc, 2)

    def plane_peer(dy, dx, dc):
        y, x, c = plane_at(dy, dx, dc)
        return {"cross": lax.div(y, 2) * 8 + x * 2 + c, "along": z * 2 + rem(y, 2)}

    def z_peer(d, y=ylo):
        return {"cross": cross, "along": rem(z + d, NZ) * 2 + y}

    def signal(sem, peer):
        pl.semaphore_signal(sem, inc=1, device_id=peer, device_id_type=MESH)

    barrier = pltpu.get_barrier_semaphore()
    first, last = cross == 0, cross == NC - 1

    @pl.when(jnp.logical_not(first))
    def _():
        signal(barrier, cross_peer(NC - 1))

    @pl.when(jnp.logical_not(last))
    def _():
        signal(barrier, cross_peer(1))

    for d in (2, NZ - 2, 1, NZ - 1):
        for y in range(2):
            signal(barrier, z_peer(d, y))
    for d in NEXT:
        signal(barrier, plane_peer(*d))

    def tell(k):
        for d in (2 << k, NZ - (2 << k)):
            signal(near.at[k], z_peer(d))
        if k == 0:
            for d in ((0, 2, 0), (2, 0, 0)):
                signal(near.at[2], plane_peer(*d))

    def hear(k):
        pl.semaphore_wait(near.at[k], 2)
        if k == 0:
            pl.semaphore_wait(near.at[2], 2)

    for copy in loads:
        copy.wait()

    lane = lax.broadcasted_iota(jnp.int32, (128, 128), 1)
    for b in range(2):
        rows = pl.ds(8 + 128 * b, 128)
        fields = [wid[rows].astype(F32)] + [fld[k, rows] for k in (1, 2, 0, 3)]
        slab = jnp.zeros((128, 128), F32)
        for k, f in enumerate(fields):
            x = pltpu.roll(jnp.where(lane < 64, f[:, :128], f[:, 128:]), 8 * (k + 1), 1)
            slab = jnp.where((lane >= 8 * k + 4) & (lane < 8 * k + 12), x, slab)
        tsl[:, :, pl.ds(128 * b, 128)] = slab.T.reshape(16, 8, 128)

    @pl.when(along == 0)
    def _():
        asl[7:11, 4:8] = jnp.zeros((4, 4, 256), F32)
        asl[11, 4:8] = jnp.ones((4, 256), F32)

    @pl.when(along == NA - 1)
    def _():
        asl[0:4, 0:4] = jnp.zeros((4, 4, 256), F32)
        asl[4, 0:4] = jnp.ones((4, 256), F32)

    for side, edge in enumerate((0, NC - 1)):

        @pl.when(cross == edge)
        def _():
            hal[0:3, side] = jnp.zeros((3, 8, 256), F32)
            hal[3, side] = jnp.ones((8, 256), F32)
            haw[side] = jnp.zeros((8, 256), jnp.int32)
            bsl[side] = jnp.zeros((16, 8, 128), F32)

    pl.semaphore_wait(barrier, len(NEXT) + 10 - jnp.where(first, 1, 0) - jnp.where(last, 1, 0))
    tell(0)

    def remote(src, dst, sems, k, peer):
        return pltpu.make_async_remote_copy(
            src_ref=src,
            dst_ref=dst,
            send_sem=sems[0].at[k],
            recv_sem=sems[1].at[k],
            device_id=peer,
            device_id_type=MESH,
        )

    cols = [
        remote(tsl.at[pl.ds(0, 5), pl.ds(4, 4)], asl.at[pl.ds(7, 5), pl.ds(4, 4)], (col_s, col_r), 0, along_peer(1)),
        remote(tsl.at[pl.ds(1, 5), pl.ds(0, 4)], asl.at[pl.ds(0, 5), pl.ds(0, 4)], (col_s, col_r), 1, along_peer(NA - 1)),
    ]
    halo = [[], []]
    for side, (src, dst, step) in enumerate(((260, 4, 1), (8, 0, NC - 1))):
        for k in (0, 1, 4, 3, 2):
            ref, to = (wid, haw) if k == 4 else (fld.at[k], hal.at[k])
            halo[side].append(
                remote(
                    ref.at[pl.ds(src, 4)], to.at[side, pl.ds(dst, 4)], (row_s, row_r), 2 * k + side, cross_peer(step)
                )
            )
    goes = (cross < NC - 1, cross > 0)
    comes = (cross > 0, cross < NC - 1)
    goes_a = (along < NA - 1, along > 0)
    comes_a = (along > 0, along < NA - 1)

    def only(cond, *acts):
        @pl.when(cond)
        def _():
            for act in acts:
                act()

    for side in range(2):
        only(goes[side], *[copy.start for copy in halo[side]])
    for side in range(2):
        only(goes_a[side], cols[side].start)

    for copy in mats:
        copy.wait()
    for src, dst in ((om, omh), (th, thh), (lm, lmh), (rm, rmh)):
        hi, lo = split(src[...])
        dst[0] = hi
        dst[1] = lo

    def coefficients(w, c):
        return w * c * ALPHA, w * (0.02 / c)

    zero8 = jnp.zeros((8, 256), F32)
    for ref in (fld.at[0], sph):
        ref[pl.ds(0, 8)] = zero8
        ref[pl.ds(264, 8)] = zero8


    def edges(f):
        lanes = lax.broadcasted_iota(jnp.int32, (CH, 128), 1)
        return jnp.where(lanes >= 96, f[:, 128:], pltpu.roll(f[:, :128], 64, 1))

    def inside(i):
        r0 = pl.multiple_of(i * CH, 8)
        here = pl.ds(r0, CH)
        own = pl.ds(pl.multiple_of(8 + i * CH, 8), CH)
        w = wid[own].astype(F32)
        e, p, q, c = (fld[k, own] for k in range(4))
        wc, fr = coefficients(w, c)
        wcs[here] = wc
        frs[here] = fr
        wp, wq = w * p, w * q
        wpx[own] = wp
        de = d12(fld[0, pl.ds(r0, CH + 16)], 0)[8 : 8 + CH]
        sph[own] = 2.0 * wp - wc * de - fr * wp
        sq = 2.0 * wq - wc * d12(e, 1) - fr * wq
        zy[here] = d12(sq, 1)
        for k, f in enumerate((w, wq, e, wc, fr)):
            edg[k, here] = edges(f)

    pl.loop(0, 256 // CH)(inside)

    @pl.loop(0, 256 // CH)
    def _(i):
        r0 = pl.multiple_of(i * CH, 8)
        zx[pl.ds(r0, CH)] = d12(sph[pl.ds(r0, CH + 16)], 0)[8 : 8 + CH]

    hear(0)
    tell(1)
    for side in range(2):
        only(comes_a[side], cols[side].wait_recv)

    corners = []
    for side, step in enumerate((1, NC - 1)):
        part = pl.ds(128 * (1 - side), 128)
        corners.append(
            [
                remote(
                    asl.at[pl.ds(tile, 3), pl.ds(row, 4), part],
                    bsl.at[side, pl.ds(tile, 3), pl.ds(row, 4)],
                    (cor_s, cor_r),
                    2 * side + k,
                    cross_peer(step),
                )
                for k, (tile, row) in enumerate(((0, 0), (7, 4)))
            ]
        )
    for side in range(2):
        only(goes[side], *[copy.start for copy in corners[side]])

    for b in range(2):
        xs[pl.ds(128 * b, 128)] = asl[:, :, pl.ds(128 * b, 128)].reshape(128, 128).T

    def beside(x, k):
        return pltpu.roll(x, 128 - 8 * k, 1) if k else x

    for side in range(2):
        only(comes[side], *[copy.wait_recv for copy in halo[side]])
    for side, at in enumerate((0, 264)):
        for k in range(4):
            fld[k, pl.ds(at, 8)] = hal[k, side]
        wid[pl.ds(at, 8)] = haw[side]

    for at, off in ((0, 0), (256, 8)):
        rows = pl.ds(at, 16)
        w = wid[rows].astype(F32)
        wc, fr = coefficients(w, fld[3, rows])
        wp = w * fld[1, rows]
        wpx[rows] = wp
        de = d12(fld[0, pl.ds(at - off, 24)], 0)[off : off + 16]
        sph[rows] = 2.0 * wp - wc * de - fr * wp
    zx[pl.ds(0, 8)] = d12(sph[pl.ds(0, 24)], 0)[8:16]
    zx[pl.ds(248, 8)] = d12(sph[pl.ds(248, 24)], 0)[8:16]

    @pl.loop(0, 256 // CHS)
    def _(i):
        here = pl.ds(pl.multiple_of(i * CHS, 8), CHS)
        own = pl.ds(pl.multiple_of(8 + i * CHS, 8), CHS)
        x = xs[here]
        lanes = lax.broadcasted_iota(jnp.int32, (CHS, 128), 1)
        w = beside(x, 0)
        wc, fr = coefficients(w, beside(x, 4))
        w, wq, e, wc, fr = (
            jnp.where(lanes < 64, new, edg[k, here])
            for k, new in enumerate((w, w * beside(x, 2), beside(x, 3), wc, fr))
        )
        dy = d12(2.0 * wq - wc * d12(e, 1) - fr * wq, 1)
        z_y = zy[here]
        z_y = jnp.concatenate(
            [
                jnp.where(lanes < 8, pltpu.roll(dy, 64, 1), z_y[:, :128]),
                jnp.where(lanes >= 120, dy, z_y[:, 128:]),
            ],
            axis=1,
        )
        en = fld[0, own] - (0.5 * ALPHA) * wid[own].astype(F32) * (zx[here] + z_y)
        sv[here] = en
        hi, lo = split(en)
        shl[0, here] = hi
        shl[1, here] = lo

    def send(n, peer, src, dst, phase, s_sem, r_sem):
        def one(d):
            pltpu.make_async_remote_copy(
                src_ref=src(d),
                dst_ref=dst(d),
                send_sem=s_sem.at[phase],
                recv_sem=r_sem.at[phase],
                device_id=peer(*d) if peer is plane_peer else peer(d),
                device_id_type=MESH,
            ).start()

        if peer is plane_peer:
            for d in PLANE:
                one(d)
            return
        one(n // 2)

        @pl.loop(1, n // 2)
        def _(s):
            one(n // 2 - s)
            one(n // 2 + s)

    def await_recv(ref, sem):
        pltpu.make_async_copy(ref, ref, sem).wait()

    def place(y, x, c):
        return y * 8 + x * 2 + c

    surf = (shl[0], shl[1])
    tr = dot3(surf, (rmh[0], rmh[1]))
    kpart[...] = dot3((lmh[0], lmh[1]), split(tr)).reshape(NA, 8, 256)
    send(NA, plane_peer, lambda d: kpart.at[place(*plane_at(*d))], lambda d: krec.at[place(*d)], 1, rs_s, rs_r)
    rpart[...] = dot3(surf, (omh[0], omh[1])).reshape(NA, 8, 128)
    cpart[...] = dot3((thh[0], thh[1]), surf).reshape(NC, 8, 256)
    hear(1)
    send(NA, along_peer, lambda d: rpart.at[rem(along + d, NA)], lambda d: rrec.at[d], 0, rs_s, rs_r)

    for side in range(2):
        only(comes[side], *[copy.wait_recv for copy in corners[side]])
    for side in range(2):
        t = bsl[side].reshape(128, 128).T
        xb[pl.ds(8 * side, 8)] = t[120:128] if side == 0 else t[0:8]

    def ring(x):
        lane = lax.broadcasted_iota(jnp.int32, x.shape, 1)
        return jnp.where(lane < 32, x, pltpu.roll(x, 64, 1))

    def e1_rows(r, n, x, lead):
        w = wid[pl.ds(r, n)].astype(F32)
        wq = jnp.concatenate([w * fld[2, pl.ds(r, n)], ring(beside(x, 0) * beside(x, 2))], axis=1)
        wp = wpx[pl.ds(pl.multiple_of(r - lead, 8), n + 16)]
        dx = d12(wp, 0)[lead : lead + n]
        dy = d12(wq, 1)[:, :256]
        e = fld[0, pl.ds(r, n)]
        return e + (e - ALPHA * w * (dx + dy))

    @pl.loop(0, 256 // CHF)
    def _(i):
        r = pl.multiple_of(8 + i * CHF, 8)
        e1x[pl.ds(r, CHF)] = e1_rows(r, CHF, xs[pl.ds(pl.multiple_of(i * CHF, 8), CHF)], 8)

    e1x[pl.ds(0, 8)] = e1_rows(0, 8, xb[pl.ds(0, 8)], 0)
    e1x[pl.ds(264, 8)] = e1_rows(264, 8, xb[pl.ds(8, 8)], 16)

    send(NC, cross_peer, lambda d: cpart.at[rem(cross + d, NC)], lambda d: crec.at[d], 2, rs_s, rs_r)

    await_recv(krec.at[pl.ds(1, NA - 1)], rs_r.at[1])
    krec[0] = kpart[plane]
    ksum[...] = jnp.sum(krec[...], axis=0)
    send(NZ, z_peer, lambda d: ksum, lambda d: zrec.at[d], 3, rs_s, rs_r)

    xb[pl.ds(16, 256)] = xs[...]

    @pl.loop(0, 256 // CHF)
    def _(i):
        r0 = pl.multiple_of(i * CHF, 8)
        r = pl.multiple_of(8 + i * CHF, 8)
        own = pl.ds(r, CHF)
        x = xs[pl.ds(r0, CHF)]
        w = wid[own].astype(F32)
        p, q = fld[1, own], fld[2, own]
        wc, fr = wcs[pl.ds(r0, CHF)], frs[pl.ds(r0, CHF)]
        p1 = p - wc * d12(fld[0, pl.ds(r0, CHF + 16)], 0)[8 : 8 + CHF] - fr * p
        ee = e1x[pl.ds(r0, CHF + 16)]
        dx = d12(ee, 0)[8 : 8 + CHF]
        pv[pl.ds(r0, CHF)] = p - 0.5 * (wc * dx + fr * (p + p1))

        hb = jnp.concatenate(
            [
                jnp.where(i == 0, xb[pl.ds(0, 8)], xb[pl.ds(pl.multiple_of(jnp.maximum(r0 + 8, 8), 8), 8)]),
                x,
                jnp.where(
                    i == 256 // CHF - 1,
                    xb[pl.ds(8, 8)],
                    xb[pl.ds(pl.multiple_of(jnp.minimum(r0 + 16 + CHF, 264), 8), 8)],
                ),
            ],
            axis=0,
        )
        wpb = ring(beside(hb, 0) * beside(hb, 1))
        dxb = d12(wpb, 0)[8 : 8 + CHF]
        wb = ring(beside(x, 0))
        wq = jnp.concatenate([w * q, ring(beside(x, 0) * beside(x, 2))], axis=1)
        dyb = d12(wq, 1)[:, 256:]
        eb = ring(beside(x, 3))
        e1b = eb + (eb - ALPHA * wb * (dxb + dyb))
        e = jnp.concatenate([fld[0, own], eb], axis=1)
        q1 = q - wc * d12(e, 1)[:, :256] - fr * q
        dy = d12(jnp.concatenate([e1x[own], e1b], axis=1), 1)[:, :256]
        qv[pl.ds(r0, CHF)] = q - 0.5 * (wc * dy + fr * (q + q1))

    await_recv(rrec.at[pl.ds(1, NA - 1)], rs_r.at[0])
    rrec[0] = rpart[along]
    rsum[z, ylo] = jnp.sum(rrec[...], axis=0)
    own_r = rsum.at[z, ylo]

    def on_z(d, k):
        pltpu.make_async_remote_copy(
            src_ref=own_r,
            dst_ref=own_r,
            send_sem=ag_s.at[0],
            recv_sem=ag_r.at[k],
            device_id=z_peer(d),
            device_id_type=MESH,
        ).start()

    for d in (8, 7, 9, 6, 10, 5, 11):
        on_z(d, 0)
    for d in (4, 12, 3, 13, 2, 14, 1, 15):
        on_z(d, 4)

    def to_pair(d):
        there = rsum.at[rem(z + d, NZ), ylo]
        pltpu.make_async_remote_copy(
            src_ref=there,
            dst_ref=there,
            send_sem=ag_s.at[3],
            recv_sem=ag_r.at[3],
            device_id={"cross": cross, "along": z * 2 + 1 - ylo},
            device_id_type=MESH,
        ).start()

    await_recv(crec.at[pl.ds(1, NC - 1)], rs_r.at[2])
    crec[0] = cpart[cross]
    csum[pl.ds(pl.multiple_of(8 * cross, 8), 8)] = jnp.sum(crec[...], axis=0)
    mine = pl.ds(pl.multiple_of(8 * cross, 8), 8)
    send(NC, cross_peer, lambda d: csum.at[mine], lambda d: csum.at[mine], 2, ag_s, ag_r)

    await_recv(zrec.at[pl.ds(1, NZ - 1)], rs_r.at[3])
    zrec[0] = ksum[...]
    total = zrec[z]
    for k in range(1, NZ):
        total = total + zrec[rem(z - k + NZ, NZ)]
    own_k = pl.ds(pl.multiple_of(8 * plane, 8), 8)
    zsum[own_k] = total
    send(NA, plane_peer, lambda d: zsum.at[own_k], lambda d: zsum.at[own_k], 1, ag_s, ag_r)

    await_recv(rsum.at[pl.ds(0, 8), 0], ag_r.at[4])
    for d in (0, 1, 15, 2, 14, 3, 13, 4, 12):
        to_pair(d)

    await_recv(csum.at[pl.ds(0, 120)], ag_r.at[2])
    await_recv(rsum.at[pl.ds(0, 7), 0], ag_r.at[0])
    for d in (5, 11, 6, 10, 7, 9, 8):
        to_pair(d)
    await_recv(zsum.at[pl.ds(0, 248)], ag_r.at[1])
    await_recv(rsum.at[:, 0], ag_r.at[3])

    for side in range(2):
        only(goes[side], *[copy.wait_send for copy in halo[side] + corners[side]])
        only(goes_a[side], cols[side].wait_send)
    await_recv(rsum.at[:, 0], ag_s.at[3])
    await_recv(rrec.at[pl.ds(1, NA - 1)], rs_s.at[0])
    await_recv(krec.at[pl.ds(1, NA - 1)], rs_s.at[1])
    await_recv(crec.at[pl.ds(1, NC - 1)], rs_s.at[2])
    await_recv(zrec.at[pl.ds(1, NZ - 1)], rs_s.at[3])
    await_recv(rsum.at[pl.ds(0, NZ - 1), 0], ag_s.at[0])
    await_recv(zsum.at[pl.ds(0, 248)], ag_s.at[1])
    await_recv(csum.at[pl.ds(0, 120)], ag_s.at[2])


def write_out(*refs):
    ins, outs, sem = refs[:6], refs[6:12], refs[12]
    copies = [pltpu.make_async_copy(a, b, sem.at[k]) for k, (a, b) in enumerate(zip(ins, outs))]
    for copy in copies:
        copy.start()
    for copy in copies:
        copy.wait()


def body(*args):
    vm = pltpu.VMEM
    dma = pltpu.SemaphoreType.DMA
    sds = jax.ShapeDtypeStruct
    held = pl.pallas_call(
        kernel,
        out_shape=(
            sds((256, 256), F32),
            sds((256, 256), F32),
            sds((256, 256), F32),
            sds((NZ, 2, 8, 128), F32),
            sds((128, 256), F32),
            sds((256, 256), F32),
        ),
        in_specs=[pl.BlockSpec(memory_space=pl.ANY)] * 9,
        out_specs=[pl.BlockSpec(memory_space=pltpu.VMEM)] * 6,
        scratch_shapes=[
            vm((4, 272, 256), F32),
            vm((272, 256), jnp.int32),
            vm((4, 2, 8, 256), F32),
            vm((2, 8, 256), jnp.int32),
            vm((16, 8, 256), F32),
            vm((16, 8, 256), F32),
            vm((2, 16, 8, 128), F32),
            vm((256, 128), F32),
            vm((272, 128), F32),
            vm((272, 256), F32),
            vm((272, 256), F32),
            vm((272, 256), F32),
            vm((256, 256), F32),
            vm((256, 256), F32),
            vm((256, 256), F32),
            vm((256, 256), F32),
            vm((5, 256, 128), F32),
            vm((2, 256, 256), BF16),
            vm((256, 128), F32),
            vm((128, 256), F32),
            vm((256, 256), F32),
            vm((256, 256), F32),
            vm((2, 256, 128), BF16),
            vm((2, 128, 256), BF16),
            vm((2, 256, 256), BF16),
            vm((2, 256, 256), BF16),
            vm((NA, 8, 128), F32),
            vm((NC, 8, 256), F32),
            vm((NA, 8, 256), F32),
            vm((NA, 8, 128), F32),
            vm((NC, 8, 256), F32),
            vm((NA, 8, 256), F32),
            vm((NZ, 8, 256), F32),
            vm((8, 256), F32),
            dma((9,)),
            dma((10,)),
            dma((10,)),
            dma((2,)),
            dma((2,)),
            dma((4,)),
            dma((4,)),
            dma((4,)),
            dma((4,)),
            dma((4,)),
            dma((5,)),
            pltpu.SemaphoreType.REGULAR((3,)),
        ],
        compiler_params=pltpu.CompilerParams(collective_id=0, has_side_effects=True, vmem_limit_bytes=16 << 20),
    )(*[pltpu.with_memory_space_constraint(a, pltpu.HBM) for a in args])
    held = held[:3] + (held[3].reshape(256, 128),) + held[4:]
    return pl.pallas_call(
        write_out,
        out_shape=tuple(sds(x.shape, F32) for x in held),
        in_specs=[pl.BlockSpec(memory_space=pltpu.VMEM)] * 6,
        out_specs=[pl.BlockSpec(memory_space=pl.ANY)] * 6,
        scratch_shapes=[dma((6,))],
        compiler_params=pltpu.CompilerParams(vmem_limit_bytes=8 << 20),
    )(*held)


def solution(mesh):
    return jax.shard_map(
        body,
        mesh=mesh,
        in_specs=(
            P("cross", "along"),
            P("cross", "along"),
            P("cross", "along"),
            P("cross", "along"),
            P("cross", "along"),
            P("along", None),
            P(None, "cross"),
            P(None, "cross"),
            P("along", None),
        ),
        out_specs=(
            P("cross", "along"),
            P("cross", "along"),
            P("cross", "along"),
            P("cross", None),
            P(None, "along"),
            P(),
        ),
        check_vma=False,
    )
```

```python
import functools

import jax
import jax.numpy as jnp
from jax import lax
from jax.experimental import pallas as pl
from jax.experimental.pallas import tpu as pltpu
from jax.sharding import PartitionSpec as P

MESH = pl.DeviceIdType.MESH
F32 = jnp.float32
BF16 = jnp.bfloat16
NC = 16
NA = 32
NZ = 16
ALPHA = 0.25 / 12.0
CH = 64
CHS = 256
CHF = 64
PLANE = sorted(
    ((dy, dx, dc) for dy in range(4) for dx in range(4) for dc in range(2) if (dy, dx, dc) != (0, 0, 0)),
    key=lambda d: -(min(d[0], 4 - d[0]) + min(d[1], 4 - d[1])),
)

NEXT = [d for d in PLANE if min(d[0], 4 - d[0]) + min(d[1], 4 - d[1]) <= 2]


def split(x):
    hi = x.astype(BF16)
    return hi, (x - hi.astype(F32)).astype(BF16)


def dot3(a, b):
    dot = functools.partial(jnp.dot, preferred_element_type=F32)
    (ah, al), (bh, bl) = a, b
    return dot(ah, bh) + (dot(ah, bl) + dot(al, bh))


def d12(f, axis):
    n = f.shape[axis]
    up1, dn1 = pltpu.roll(f, n - 1, axis), pltpu.roll(f, 1, axis)
    up2, dn2 = pltpu.roll(f, n - 2, axis), pltpu.roll(f, 2, axis)
    return 8.0 * (up1 - dn1) - (up2 - dn2)


def kernel(
    e_in, p_in, q_in, c_in, w_in, om_in, th_in, l_in, r_in,
    sv, pv, qv, rsum, csum, zsum,
    fld, wid, hal, haw, tsl, asl, bsl, xs, xb, sph, wpx, e1x, wcs, frs, zx, zy, edg, shl,
    om, th, lm, rm, omh, thh, lmh, rmh,
    rpart, cpart, kpart, rrec, crec, krec, zrec, ksum,
    in_sem, row_s, row_r, col_s, col_r, cor_s, cor_r,
    rs_s, rs_r, ag_s, ag_r, near,
):
    cross = lax.axis_index("cross")
    along = lax.axis_index("along")
    z, ylo = along // 2, along % 2
    yhi, x_at, core = cross // 8, cross // 2 % 4, cross % 2
    y_at = yhi * 2 + ylo
    plane = y_at * 8 + x_at * 2 + core

    loads = [
        pltpu.make_async_copy(src, fld.at[k, pl.ds(8, 256)], in_sem.at[k])
        for k, src in enumerate((e_in, p_in, q_in, c_in))
    ]
    loads.append(pltpu.make_async_copy(w_in, wid.at[pl.ds(8, 256)], in_sem.at[4]))
    for copy in loads:
        copy.start()
    mats = [
        pltpu.make_async_copy(src, dst, in_sem.at[5 + k])
        for k, (src, dst) in enumerate(((om_in, om), (th_in, th), (l_in, lm), (r_in, rm)))
    ]
    for copy in mats:
        copy.start()

    rem = lax.rem

    def along_peer(d):
        return {"cross": cross, "along": rem(along + d, NA)}

    def cross_peer(d):
        return {"cross": rem(cross + d, NC), "along": along}

    def plane_at(dy, dx, dc):
        return rem(y_at + dy, 4), rem(x_at + dx, 4), rem(core + dc, 2)

    def plane_peer(dy, dx, dc):
        y, x, c = plane_at(dy, dx, dc)
        return {"cross": lax.div(y, 2) * 8 + x * 2 + c, "along": z * 2 + rem(y, 2)}

    def z_peer(d, y=ylo):
        return {"cross": cross, "along": rem(z + d, NZ) * 2 + y}

    def signal(sem, peer):
        pl.semaphore_signal(sem, inc=1, device_id=peer, device_id_type=MESH)

    barrier = pltpu.get_barrier_semaphore()
    first, last = cross == 0, cross == NC - 1

    @pl.when(jnp.logical_not(first))
    def _():
        signal(barrier, cross_peer(NC - 1))

    @pl.when(jnp.logical_not(last))
    def _():
        signal(barrier, cross_peer(1))

    for d in (2, NZ - 2, 1, NZ - 1):
        for y in range(2):
            signal(barrier, z_peer(d, y))
    for d in NEXT:
        signal(barrier, plane_peer(*d))

    def tell(k):
        for d in (2 << k, NZ - (2 << k)):
            signal(near.at[k], z_peer(d))
        if k == 0:
            for d in ((0, 2, 0), (2, 0, 0)):
                signal(near.at[2], plane_peer(*d))

    def hear(k):
        pl.semaphore_wait(near.at[k], 2)
        if k == 0:
            pl.semaphore_wait(near.at[2], 2)

    for copy in loads:
        copy.wait()

    lane = lax.broadcasted_iota(jnp.int32, (128, 128), 1)
    for b in range(2):
        rows = pl.ds(8 + 128 * b, 128)
        fields = [wid[rows].astype(F32)] + [fld[k, rows] for k in (1, 2, 0, 3)]
        slab = jnp.zeros((128, 128), F32)
        for k, f in enumerate(fields):
            x = pltpu.roll(jnp.where(lane < 64, f[:, :128], f[:, 128:]), 8 * (k + 1), 1)
            slab = jnp.where((lane >= 8 * k + 4) & (lane < 8 * k + 12), x, slab)
        tsl[:, :, pl.ds(128 * b, 128)] = slab.T.reshape(16, 8, 128)

    @pl.when(along == 0)
    def _():
        asl[7:11, 4:8] = jnp.zeros((4, 4, 256), F32)
        asl[11, 4:8] = jnp.ones((4, 256), F32)

    @pl.when(along == NA - 1)
    def _():
        asl[0:4, 0:4] = jnp.zeros((4, 4, 256), F32)
        asl[4, 0:4] = jnp.ones((4, 256), F32)

    for side, edge in enumerate((0, NC - 1)):

        @pl.when(cross == edge)
        def _():
            hal[0:3, side] = jnp.zeros((3, 8, 256), F32)
            hal[3, side] = jnp.ones((8, 256), F32)
            haw[side] = jnp.zeros((8, 256), jnp.int32)
            bsl[side] = jnp.zeros((16, 8, 128), F32)

    pl.semaphore_wait(barrier, len(NEXT) + 10 - jnp.where(first, 1, 0) - jnp.where(last, 1, 0))
    tell(0)

    def remote(src, dst, sems, k, peer):
        return pltpu.make_async_remote_copy(
            src_ref=src,
            dst_ref=dst,
            send_sem=sems[0].at[k],
            recv_sem=sems[1].at[k],
            device_id=peer,
            device_id_type=MESH,
        )

    cols = [
        remote(tsl.at[pl.ds(0, 5), pl.ds(4, 4)], asl.at[pl.ds(7, 5), pl.ds(4, 4)], (col_s, col_r), 0, along_peer(1)),
        remote(tsl.at[pl.ds(1, 5), pl.ds(0, 4)], asl.at[pl.ds(0, 5), pl.ds(0, 4)], (col_s, col_r), 1, along_peer(NA - 1)),
    ]
    halo = [[], []]
    for side, (src, dst, step) in enumerate(((260, 4, 1), (8, 0, NC - 1))):
        for k in (0, 1, 4, 3, 2):
            ref, to = (wid, haw) if k == 4 else (fld.at[k], hal.at[k])
            halo[side].append(
                remote(
                    ref.at[pl.ds(src, 4)], to.at[side, pl.ds(dst, 4)], (row_s, row_r), 2 * k + side, cross_peer(step)
                )
            )
    goes = (cross < NC - 1, cross > 0)
    comes = (cross > 0, cross < NC - 1)
    goes_a = (along < NA - 1, along > 0)
    comes_a = (along > 0, along < NA - 1)

    def only(cond, *acts):
        @pl.when(cond)
        def _():
            for act in acts:
                act()

    for side in range(2):
        only(goes[side], *[copy.start for copy in halo[side]])
    for side in range(2):
        only(goes_a[side], cols[side].start)

    for copy in mats:
        copy.wait()
    for src, dst in ((om, omh), (th, thh), (lm, lmh), (rm, rmh)):
        hi, lo = split(src[...])
        dst[0] = hi
        dst[1] = lo

    def coefficients(w, c):
        return w * c * ALPHA, w * (0.02 / c)

    zero8 = jnp.zeros((8, 256), F32)
    for ref in (fld.at[0], sph):
        ref[pl.ds(0, 8)] = zero8
        ref[pl.ds(264, 8)] = zero8


    def edges(f):
        lanes = lax.broadcasted_iota(jnp.int32, (CH, 128), 1)
        return jnp.where(lanes >= 96, f[:, 128:], pltpu.roll(f[:, :128], 64, 1))

    def inside(i):
        r0 = pl.multiple_of(i * CH, 8)
        here = pl.ds(r0, CH)
        own = pl.ds(pl.multiple_of(8 + i * CH, 8), CH)
        w = wid[own].astype(F32)
        e, p, q, c = (fld[k, own] for k in range(4))
        wc, fr = coefficients(w, c)
        wcs[here] = wc
        frs[here] = fr
        wp, wq = w * p, w * q
        wpx[own] = wp
        de = d12(fld[0, pl.ds(r0, CH + 16)], 0)[8 : 8 + CH]
        sph[own] = 2.0 * wp - wc * de - fr * wp
        sq = 2.0 * wq - wc * d12(e, 1) - fr * wq
        zy[here] = d12(sq, 1)
        for k, f in enumerate((w, wq, e, wc, fr)):
            edg[k, here] = edges(f)

    pl.loop(0, 256 // CH)(inside)

    @pl.loop(0, 256 // CH)
    def _(i):
        r0 = pl.multiple_of(i * CH, 8)
        zx[pl.ds(r0, CH)] = d12(sph[pl.ds(r0, CH + 16)], 0)[8 : 8 + CH]

    hear(0)
    tell(1)
    for side in range(2):
        only(comes_a[side], cols[side].wait_recv)

    corners = []
    for side, step in enumerate((1, NC - 1)):
        part = pl.ds(128 * (1 - side), 128)
        corners.append(
            [
                remote(
                    asl.at[pl.ds(tile, 3), pl.ds(row, 4), part],
                    bsl.at[side, pl.ds(tile, 3), pl.ds(row, 4)],
                    (cor_s, cor_r),
                    2 * side + k,
                    cross_peer(step),
                )
                for k, (tile, row) in enumerate(((0, 0), (7, 4)))
            ]
        )
    for side in range(2):
        only(goes[side], *[copy.start for copy in corners[side]])

    for b in range(2):
        xs[pl.ds(128 * b, 128)] = asl[:, :, pl.ds(128 * b, 128)].reshape(128, 128).T

    def beside(x, k):
        return pltpu.roll(x, 128 - 8 * k, 1) if k else x

    for side in range(2):
        only(comes[side], *[copy.wait_recv for copy in halo[side]])
    for side, at in enumerate((0, 264)):
        for k in range(4):
            fld[k, pl.ds(at, 8)] = hal[k, side]
        wid[pl.ds(at, 8)] = haw[side]

    for at, off in ((0, 0), (256, 8)):
        rows = pl.ds(at, 16)
        w = wid[rows].astype(F32)
        wc, fr = coefficients(w, fld[3, rows])
        wp = w * fld[1, rows]
        wpx[rows] = wp
        de = d12(fld[0, pl.ds(at - off, 24)], 0)[off : off + 16]
        sph[rows] = 2.0 * wp - wc * de - fr * wp
    zx[pl.ds(0, 8)] = d12(sph[pl.ds(0, 24)], 0)[8:16]
    zx[pl.ds(248, 8)] = d12(sph[pl.ds(248, 24)], 0)[8:16]

    @pl.loop(0, 256 // CHS)
    def _(i):
        here = pl.ds(pl.multiple_of(i * CHS, 8), CHS)
        own = pl.ds(pl.multiple_of(8 + i * CHS, 8), CHS)
        x = xs[here]
        lanes = lax.broadcasted_iota(jnp.int32, (CHS, 128), 1)
        w = beside(x, 0)
        wc, fr = coefficients(w, beside(x, 4))
        w, wq, e, wc, fr = (
            jnp.where(lanes < 64, new, edg[k, here])
            for k, new in enumerate((w, w * beside(x, 2), beside(x, 3), wc, fr))
        )
        dy = d12(2.0 * wq - wc * d12(e, 1) - fr * wq, 1)
        z_y = zy[here]
        z_y = jnp.concatenate(
            [
                jnp.where(lanes < 8, pltpu.roll(dy, 64, 1), z_y[:, :128]),
                jnp.where(lanes >= 120, dy, z_y[:, 128:]),
            ],
            axis=1,
        )
        en = fld[0, own] - (0.5 * ALPHA) * wid[own].astype(F32) * (zx[here] + z_y)
        sv[here] = en
        hi, lo = split(en)
        shl[0, here] = hi
        shl[1, here] = lo

    def send(n, peer, src, dst, phase, s_sem, r_sem):
        def one(d):
            pltpu.make_async_remote_copy(
                src_ref=src(d),
                dst_ref=dst(d),
                send_sem=s_sem.at[phase],
                recv_sem=r_sem.at[phase],
                device_id=peer(*d) if peer is plane_peer else peer(d),
                device_id_type=MESH,
            ).start()

        if peer is plane_peer:
            for d in PLANE:
                one(d)
            return
        one(n // 2)

        @pl.loop(1, n // 2)
        def _(s):
            one(n // 2 - s)
            one(n // 2 + s)

    def await_recv(ref, sem):
        pltpu.make_async_copy(ref, ref, sem).wait()

    def place(y, x, c):
        return y * 8 + x * 2 + c

    surf = (shl[0], shl[1])
    tr = dot3(surf, (rmh[0], rmh[1]))
    kpart[...] = dot3((lmh[0], lmh[1]), split(tr)).reshape(NA, 8, 256)
    send(NA, plane_peer, lambda d: kpart.at[place(*plane_at(*d))], lambda d: krec.at[place(*d)], 1, rs_s, rs_r)
    rpart[...] = dot3(surf, (omh[0], omh[1])).reshape(NA, 8, 128)
    cpart[...] = dot3((thh[0], thh[1]), surf).reshape(NC, 8, 256)
    hear(1)
    send(NA, along_peer, lambda d: rpart.at[rem(along + d, NA)], lambda d: rrec.at[d], 0, rs_s, rs_r)

    for side in range(2):
        only(comes[side], *[copy.wait_recv for copy in corners[side]])
    for side in range(2):
        t = bsl[side].reshape(128, 128).T
        xb[pl.ds(8 * side, 8)] = t[120:128] if side == 0 else t[0:8]

    def ring(x):
        lane = lax.broadcasted_iota(jnp.int32, x.shape, 1)
        return jnp.where(lane < 32, x, pltpu.roll(x, 64, 1))

    def e1_rows(r, n, x, lead):
        w = wid[pl.ds(r, n)].astype(F32)
        wq = jnp.concatenate([w * fld[2, pl.ds(r, n)], ring(beside(x, 0) * beside(x, 2))], axis=1)
        wp = wpx[pl.ds(pl.multiple_of(r - lead, 8), n + 16)]
        dx = d12(wp, 0)[lead : lead + n]
        dy = d12(wq, 1)[:, :256]
        e = fld[0, pl.ds(r, n)]
        return e + (e - ALPHA * w * (dx + dy))

    @pl.loop(0, 256 // CHF)
    def _(i):
        r = pl.multiple_of(8 + i * CHF, 8)
        e1x[pl.ds(r, CHF)] = e1_rows(r, CHF, xs[pl.ds(pl.multiple_of(i * CHF, 8), CHF)], 8)

    e1x[pl.ds(0, 8)] = e1_rows(0, 8, xb[pl.ds(0, 8)], 0)
    e1x[pl.ds(264, 8)] = e1_rows(264, 8, xb[pl.ds(8, 8)], 16)

    send(NC, cross_peer, lambda d: cpart.at[rem(cross + d, NC)], lambda d: crec.at[d], 2, rs_s, rs_r)

    await_recv(krec.at[pl.ds(1, NA - 1)], rs_r.at[1])
    krec[0] = kpart[plane]
    ksum[...] = jnp.sum(krec[...], axis=0)

    @pl.loop(0, NZ - 1)
    def _(k):
        d = rem(k + jnp.where(k >= z, 1, 0) - z + NZ, NZ)
        remote(ksum, zrec.at[d], (rs_s, rs_r), 3, z_peer(d)).start()


    xb[pl.ds(16, 256)] = xs[...]

    @pl.loop(0, 256 // CHF)
    def _(i):
        r0 = pl.multiple_of(i * CHF, 8)
        r = pl.multiple_of(8 + i * CHF, 8)
        own = pl.ds(r, CHF)
        x = xs[pl.ds(r0, CHF)]
        w = wid[own].astype(F32)
        p, q = fld[1, own], fld[2, own]
        wc, fr = wcs[pl.ds(r0, CHF)], frs[pl.ds(r0, CHF)]
        p1 = p - wc * d12(fld[0, pl.ds(r0, CHF + 16)], 0)[8 : 8 + CHF] - fr * p
        ee = e1x[pl.ds(r0, CHF + 16)]
        dx = d12(ee, 0)[8 : 8 + CHF]
        pv[pl.ds(r0, CHF)] = p - 0.5 * (wc * dx + fr * (p + p1))

        hb = jnp.concatenate(
            [
                jnp.where(i == 0, xb[pl.ds(0, 8)], xb[pl.ds(pl.multiple_of(jnp.maximum(r0 + 8, 8), 8), 8)]),
                x,
                jnp.where(
                    i == 256 // CHF - 1,
                    xb[pl.ds(8, 8)],
                    xb[pl.ds(pl.multiple_of(jnp.minimum(r0 + 16 + CHF, 264), 8), 8)],
                ),
            ],
            axis=0,
        )
        wpb = ring(beside(hb, 0) * beside(hb, 1))
        dxb = d12(wpb, 0)[8 : 8 + CHF]
        wb = ring(beside(x, 0))
        wq = jnp.concatenate([w * q, ring(beside(x, 0) * beside(x, 2))], axis=1)
        dyb = d12(wq, 1)[:, 256:]
        eb = ring(beside(x, 3))
        e1b = eb + (eb - ALPHA * wb * (dxb + dyb))
        e = jnp.concatenate([fld[0, own], eb], axis=1)
        q1 = q - wc * d12(e, 1)[:, :256] - fr * q
        dy = d12(jnp.concatenate([e1x[own], e1b], axis=1), 1)[:, :256]
        qv[pl.ds(r0, CHF)] = q - 0.5 * (wc * dy + fr * (q + q1))

    await_recv(rrec.at[pl.ds(1, NA - 1)], rs_r.at[0])
    rrec[0] = rpart[along]
    rsum[z, ylo] = jnp.sum(rrec[...], axis=0)
    own_r = rsum.at[z, ylo]

    def on_z(d, k):
        pltpu.make_async_remote_copy(
            src_ref=own_r,
            dst_ref=own_r,
            send_sem=ag_s.at[0],
            recv_sem=ag_r.at[k],
            device_id=z_peer(d),
            device_id_type=MESH,
        ).start()

    for d in (8, 7, 9, 6, 10, 5, 11):
        on_z(d, 0)
    for d in (4, 12, 3, 13, 2, 14, 1, 15):
        on_z(d, 4)

    def to_pair(d):
        there = rsum.at[rem(z + d, NZ), ylo]
        pltpu.make_async_remote_copy(
            src_ref=there,
            dst_ref=there,
            send_sem=ag_s.at[3],
            recv_sem=ag_r.at[3],
            device_id={"cross": cross, "along": z * 2 + 1 - ylo},
            device_id_type=MESH,
        ).start()

    await_recv(crec.at[pl.ds(1, NC - 1)], rs_r.at[2])
    crec[0] = cpart[cross]
    csum[pl.ds(pl.multiple_of(8 * cross, 8), 8)] = jnp.sum(crec[...], axis=0)
    mine = pl.ds(pl.multiple_of(8 * cross, 8), 8)
    send(NC, cross_peer, lambda d: csum.at[mine], lambda d: csum.at[mine], 2, ag_s, ag_r)

    await_recv(zrec.at[pl.ds(1, NZ - 1)], rs_r.at[3])
    zrec[0] = ksum[...]
    total = zrec[z]
    for k in range(1, NZ):
        total = total + zrec[rem(z - k + NZ, NZ)]
    own_k = pl.ds(pl.multiple_of(8 * plane, 8), 8)
    zsum[own_k] = total
    send(NA, plane_peer, lambda d: zsum.at[own_k], lambda d: zsum.at[own_k], 1, ag_s, ag_r)

    await_recv(rsum.at[pl.ds(0, 8), 0], ag_r.at[4])
    for d in (0, 1, 15, 2, 14, 3, 13, 4, 12):
        to_pair(d)

    await_recv(csum.at[pl.ds(0, 120)], ag_r.at[2])
    await_recv(rsum.at[pl.ds(0, 7), 0], ag_r.at[0])
    for d in (5, 11, 6, 10, 7, 9, 8):
        to_pair(d)
    await_recv(zsum.at[pl.ds(0, 248)], ag_r.at[1])
    await_recv(rsum.at[:, 0], ag_r.at[3])

    for side in range(2):
        only(goes[side], *[copy.wait_send for copy in halo[side] + corners[side]])
        only(goes_a[side], cols[side].wait_send)
    await_recv(rsum.at[:, 0], ag_s.at[3])
    await_recv(rrec.at[pl.ds(1, NA - 1)], rs_s.at[0])
    await_recv(krec.at[pl.ds(1, NA - 1)], rs_s.at[1])
    await_recv(crec.at[pl.ds(1, NC - 1)], rs_s.at[2])
    await_recv(zrec.at[pl.ds(1, NZ - 1)], rs_s.at[3])
    await_recv(rsum.at[pl.ds(0, NZ - 1), 0], ag_s.at[0])
    await_recv(zsum.at[pl.ds(0, 248)], ag_s.at[1])
    await_recv(csum.at[pl.ds(0, 120)], ag_s.at[2])


def write_out(*refs):
    ins, outs, sem = refs[:6], refs[6:12], refs[12]
    copies = [pltpu.make_async_copy(a, b, sem.at[k]) for k, (a, b) in enumerate(zip(ins, outs))]
    for copy in copies:
        copy.start()
    for copy in copies:
        copy.wait()


def body(*args):
    vm = pltpu.VMEM
    dma = pltpu.SemaphoreType.DMA
    sds = jax.ShapeDtypeStruct
    held = pl.pallas_call(
        kernel,
        out_shape=(
            sds((256, 256), F32),
            sds((256, 256), F32),
            sds((256, 256), F32),
            sds((NZ, 2, 8, 128), F32),
            sds((128, 256), F32),
            sds((256, 256), F32),
        ),
        in_specs=[pl.BlockSpec(memory_space=pl.ANY)] * 9,
        out_specs=[pl.BlockSpec(memory_space=pltpu.VMEM)] * 6,
        scratch_shapes=[
            vm((4, 272, 256), F32),
            vm((272, 256), jnp.int32),
            vm((4, 2, 8, 256), F32),
            vm((2, 8, 256), jnp.int32),
            vm((16, 8, 256), F32),
            vm((16, 8, 256), F32),
            vm((2, 16, 8, 128), F32),
            vm((256, 128), F32),
            vm((272, 128), F32),
            vm((272, 256), F32),
            vm((272, 256), F32),
            vm((272, 256), F32),
            vm((256, 256), F32),
            vm((256, 256), F32),
            vm((256, 256), F32),
            vm((256, 256), F32),
            vm((5, 256, 128), F32),
            vm((2, 256, 256), BF16),
            vm((256, 128), F32),
            vm((128, 256), F32),
            vm((256, 256), F32),
            vm((256, 256), F32),
            vm((2, 256, 128), BF16),
            vm((2, 128, 256), BF16),
            vm((2, 256, 256), BF16),
            vm((2, 256, 256), BF16),
            vm((NA, 8, 128), F32),
            vm((NC, 8, 256), F32),
            vm((NA, 8, 256), F32),
            vm((NA, 8, 128), F32),
            vm((NC, 8, 256), F32),
            vm((NA, 8, 256), F32),
            vm((NZ, 8, 256), F32),
            vm((8, 256), F32),
            dma((9,)),
            dma((10,)),
            dma((10,)),
            dma((2,)),
            dma((2,)),
            dma((4,)),
            dma((4,)),
            dma((4,)),
            dma((4,)),
            dma((4,)),
            dma((5,)),
            pltpu.SemaphoreType.REGULAR((3,)),
        ],
        compiler_params=pltpu.CompilerParams(collective_id=0, has_side_effects=True, vmem_limit_bytes=16 << 20),
    )(*[pltpu.with_memory_space_constraint(a, pltpu.HBM) for a in args])
    held = held[:3] + (held[3].reshape(256, 128),) + held[4:]
    return pl.pallas_call(
        write_out,
        out_shape=tuple(sds(x.shape, F32) for x in held),
        in_specs=[pl.BlockSpec(memory_space=pltpu.VMEM)] * 6,
        out_specs=[pl.BlockSpec(memory_space=pl.ANY)] * 6,
        scratch_shapes=[dma((6,))],
        compiler_params=pltpu.CompilerParams(vmem_limit_bytes=8 << 20),
    )(*held)


def solution(mesh):
    return jax.shard_map(
        body,
        mesh=mesh,
        in_specs=(
            P("cross", "along"),
            P("cross", "along"),
            P("cross", "along"),
            P("cross", "along"),
            P("cross", "along"),
            P("along", None),
            P(None, "cross"),
            P(None, "cross"),
            P("along", None),
        ),
        out_specs=(
            P("cross", "along"),
            P("cross", "along"),
            P("cross", "along"),
            P("cross", None),
            P(None, "along"),
            P(),
        ),
        check_vma=False,
    )
```
